256 devices in a mesh: seq: 32 (over z, y), head: 8 (over x, core).
Axes of the slice: x: 4, y: 4, z: 8, core: 2. Of those that a mesh axis runs over, the one named last changes fastest.
Arguments:
- query: bfloat16 [32768, 4096], P('seq', 'head'), may hold values from -0.15625 to 0.15625
- key: bfloat16 [32768, 4096], P('seq', 'head'), may hold values from -0.15625 to 0.15625
- value: bfloat16 [32768, 4096], P('seq', 'head'), may hold values from -18 to 18, as said below
- level_coef: float32 [6, 32, 32768], P(None, 'head', 'seq'), may hold values from 0.25 to 2.5
- gain: float32 [4096], P('head'), may hold values from 0.5 to 1.5
- cotangent: bfloat16 [32768, 4096], P('seq', 'head'), may hold values from -0.625 to 0.625
Outputs:
- mixed: bfloat16 [32768, 4096], P('seq', 'head')
- grad_query: bfloat16 [32768, 4096], P('seq', 'head')
- grad_key: bfloat16 [32768, 4096], P('seq', 'head')
- grad_value: bfloat16 [32768, 4096], P('seq', 'head')
- grad_level: float32 [6, 32, 32768], P(None, 'head', 'seq')
- grad_gain: float32 [4096], P('head')
The draws below stay inside these ranges and needn't reach their ends.
Inputs may be any that keep to these rules, and one draw needn't show every extreme that they name: `value`: real values.
All inputs are finite; a program needn't handle non-finite values.
Results may differ from the reference program's by a relative error of at most 0.0065.
Values sent between devices are 32-bit elements; how exact they have to be, the bound alone decides.
A program may use at most 128 MiB of HBM per device.

```python
import math
import jax
import jax.numpy as jnp
from jax import lax

HEADS = 32
HEAD_DIM = 128
TOK_DEV = 1024
TOKENS = 32768
LEVELS = 6
N_SEQ = 32


def draw_value(key, part):
    first = jax.random.fold_in(jax.random.fold_in(key, 7), 0)
    columns = jnp.arange(HEADS * HEAD_DIM, dtype=jnp.int32) // HEAD_DIM
    scale = 1.0 + 2.0 * columns.astype(jnp.float32) / max(HEADS - 1, 1)
    base = jnp.clip(jax.random.normal(first, (TOKENS, HEADS * HEAD_DIM), jnp.float32), -6.0, 6.0)
    return (base * scale[None, :]).astype(jnp.bfloat16)


def level_of(own_key, extent, cuts, low, largest):
    level = 1.0
    for position, blocks in cuts:
        heights = jax.random.uniform(jax.random.fold_in(jax.random.fold_in(own_key, 6), position), (blocks,), jnp.float32, low / len(cuts), largest / len(cuts))
        level = level * jnp.repeat(jnp.exp(heights), extent[position] // blocks).reshape((-1,) + (1,) * (len(extent) - 1 - position))
    return level


def normal_values(own_key, dims, deviation, most, pieces=(), kind=jnp.bfloat16):
    values = jax.random.normal(own_key, dims, jnp.float32) * deviation
    if len(pieces) > 0:
        values = level_of(own_key, dims, pieces, -0.22, 0.18) * values
    return jnp.clip(values, min=-most, max=most).astype(kind)


def setup_inputs(seed: int = 0) -> dict:
    key_of = jax.random.split(jax.random.key(seed), 7)
    query = normal_values(key_of[0], (TOKENS, HEADS * HEAD_DIM), 0.026, 0.15625, ((0, 32), (1, 8)))
    key = normal_values(key_of[1], (TOKENS, HEADS * HEAD_DIM), 0.026, 0.15625, ((0, 32), (1, 8)))
    value = draw_value(jax.random.fold_in(key_of[6], 71), 0)
    level_coef = jnp.clip(jnp.exp(math.log(2.5) - 2.3025851 * jax.random.uniform(key_of[3], (LEVELS, HEADS, TOKENS), jnp.float32) ** level_of(key_of[3], (LEVELS, HEADS, TOKENS), ((1, 8), (2, 32)), -0.2, 0.2)), 0.25, 2.5)
    gain = jnp.clip(1.0 + 0.1 * jax.random.normal(key_of[4], (HEADS * HEAD_DIM,), jnp.float32), 0.5, 1.5)
    cotangent = normal_values(key_of[5], (TOKENS, HEADS * HEAD_DIM), 0.1, 0.625, ((0, 32), (1, 8)))
    return {"query": query, "key": key, "value": value, "level_coef": level_coef, "gain": gain, "cotangent": cotangent}


EPS = 1e-06

def sibling_sums(states, level):
    count = states.shape[0]
    span = 2 ** level
    blocks = states.reshape((count // span, span) + states.shape[1:]).sum(axis=1)
    pairs = blocks.reshape((count // (2 * span), 2) + blocks.shape[1:])
    flipped = pairs[:, ::-1].reshape(blocks.shape)
    return jnp.repeat(flipped, span, axis=0)

def causal_scores(query, key):
    size = query.shape[0]
    scores = jnp.einsum('the,she->hts', query.astype(jnp.float32), key.astype(jnp.float32))
    causal = jnp.arange(size, dtype=jnp.int32)[:, None] >= jnp.arange(size, dtype=jnp.int32)[None, :]
    return (jnp.where(causal[None], scores, 0.0).astype(jnp.bfloat16).astype(jnp.float32), causal)

def forward_group(query, key, value, coef, buckets):
    kept, causal = causal_scores(query, key)
    local = jnp.einsum('hts,she->the', kept, value.astype(jnp.float32))
    reads = jnp.einsum('the,lhef->lthf', query.astype(jnp.float32), buckets.astype(jnp.float32))
    total = coef[0].T[:, :, None] * local
    total = total + lax.optimization_barrier(jnp.sum(coef[1:].transpose(0, 2, 1)[..., None] * reads, axis=0))
    return total

def backward_group(query, key, value, coef, buckets, grad_out):
    qf = query.astype(jnp.float32)
    kf = key.astype(jnp.float32)
    vf = value.astype(jnp.float32)
    bf = buckets.astype(jnp.float32)
    dof = grad_out.astype(jnp.float32)
    kept, causal = causal_scores(query, key)
    local = jnp.einsum('hts,she->the', kept, vf)
    first = coef[0].T[:, :, None]
    reads = jnp.einsum('the,lhef->lthf', qf, bf)
    grad_first = lax.optimization_barrier(jnp.sum(dof * local, axis=-1))
    grad_rest = lax.optimization_barrier(jnp.sum(dof[None] * reads, axis=-1))
    grad_coef = jnp.concatenate([grad_first.T[None], grad_rest.transpose(0, 2, 1)], axis=0)
    weighted = (first * dof).astype(jnp.bfloat16).astype(jnp.float32)
    grad_value = jnp.einsum('hts,the->she', kept, weighted)
    pair = jnp.einsum('the,she->hts', dof, vf) * coef[0][:, :, None]
    pair = jnp.where(causal[None], pair, 0.0).astype(jnp.bfloat16).astype(jnp.float32)
    grad_query = jnp.einsum('hts,she->the', pair, kf)
    grad_key = jnp.einsum('hts,the->she', pair, qf)
    scaled = (coef[1:].transpose(0, 2, 1)[..., None] * dof[None]).astype(jnp.bfloat16).astype(jnp.float32)
    grad_query = grad_query + jnp.einsum('lthf,lhef->the', scaled, bf)
    grad_buckets = jnp.einsum('the,lthf->lhef', qf, scaled)
    return (grad_query, grad_key, grad_value, grad_coef, grad_buckets)

def reference(query, key, value, level_coef, gain, cotangent):
    count = N_SEQ
    size = TOK_DEV
    shape4 = (count, size, HEADS, HEAD_DIM)
    q4 = query.reshape(shape4)
    k4 = key.reshape(shape4)
    v4 = value.reshape(shape4)
    c4 = cotangent.reshape(shape4)
    coef = level_coef.reshape(LEVELS, HEADS, count, size).transpose(2, 0, 1, 3)
    states = jnp.einsum('ncha,nchb->nhab', k4.astype(jnp.float32), v4.astype(jnp.float32))
    groups = jnp.arange(count, dtype=jnp.int32)
    found = []
    for level in range(LEVELS - 1):
        bit = (groups // 2 ** level % 2).astype(jnp.float32)
        found.append(bit[:, None, None, None] * sibling_sums(states, level))
    bucket_half = jnp.stack(found, axis=1).astype(jnp.bfloat16)
    output = lax.map(lambda parts: forward_group(*parts), (q4, k4, v4, coef, bucket_half))
    total = lax.optimization_barrier(jnp.mean(output * output, axis=(2, 3)))
    root = jnp.sqrt(total + EPS)[..., None, None]
    normed = output / root
    gain2 = gain.reshape(HEADS, HEAD_DIM)
    mixed = (normed * gain2).astype(jnp.bfloat16).reshape(TOKENS, HEADS * HEAD_DIM)
    cot = c4.astype(jnp.float32)
    grad_gain = lax.optimization_barrier(jnp.sum(cot * normed, axis=(0, 1))).reshape(-1)
    scaled = cot * gain2
    inner = lax.optimization_barrier(jnp.sum(scaled * output, axis=(2, 3)))[..., None, None]
    grad_out = ((scaled - output * inner / (HEADS * HEAD_DIM * root * root)) / root).astype(jnp.bfloat16)
    q_grad, k_grad, v_grad, coef_grad, bucket_grad = lax.map(lambda parts: backward_group(*parts), (q4, k4, v4, coef, bucket_half, grad_out))
    carried = jnp.zeros_like(states)
    for level in range(LEVELS - 1):
        bit = (groups // 2 ** level % 2).astype(jnp.float32)
        carried = carried + sibling_sums(bit[:, None, None, None] * bucket_grad[:, level], level)
    grad_states = carried.astype(jnp.bfloat16).astype(jnp.float32)
    k_grad = k_grad + jnp.einsum('nshb,nhab->nsha', v4.astype(jnp.float32), grad_states)
    v_grad = v_grad + jnp.einsum('nsha,nhab->nshb', k4.astype(jnp.float32), grad_states)
    flat = (TOKENS, HEADS * HEAD_DIM)
    grad_query = q_grad.astype(jnp.bfloat16).reshape(flat)
    grad_key = k_grad.astype(jnp.bfloat16).reshape(flat)
    grad_value = v_grad.astype(jnp.bfloat16).reshape(flat)
    grad_level = coef_grad.transpose(1, 2, 0, 3).reshape(LEVELS, HEADS, TOKENS)
    return (mixed, grad_query, grad_key, grad_value, grad_level, grad_gain)
```

```python
import jax
import jax.numpy as jnp
from jax import lax
from jax.experimental import pallas as pl
from jax.experimental.pallas import tpu as pltpu
from jax.sharding import PartitionSpec as P

EPS = 1e-06
F32 = jnp.float32
BF16 = jnp.bfloat16
MESH = pl.DeviceIdType.MESH

NY = 4
NZ = 8
NH = 8
HL = 4
D = 128
T = 1024
C = 256
NC = T // C
SUB = D // NZ


def dot_nn(a, b):
    return lax.dot_general(a, b, (((1,), (0,)), ((), ())), preferred_element_type=F32)


def dot_nt(a, b):
    return lax.dot_general(a, b, (((1,), (1,)), ((), ())), preferred_element_type=F32)


def dot_tn(a, b):
    return lax.dot_general(a, b, (((0,), (0,)), ((), ())), preferred_element_type=F32)


def head_lanes(h):
    return slice(h * D, (h + 1) * D)


def chunk_rows(c, size=C):
    return pl.ds(pl.multiple_of(c * size, size), size)


def when(cond, fn):
    if cond is True:
        fn()
    elif cond is not False:
        pl.when(cond)(fn)


SCRATCH = dict(
    q=pltpu.VMEM((T, HL * D), BF16),
    k=pltpu.VMEM((T, HL * D), BF16),
    v=pltpu.VMEM((T, HL * D), BF16),
    cot=pltpu.VMEM((T, HL * D), BF16),
    lam=pltpu.VMEM((6, HL, T), F32),
    gain=pltpu.VMEM((1, HL * D), F32),
    mixed=pltpu.VMEM((T, HL * D), BF16),
    gq=pltpu.VMEM((T, HL * D), BF16),
    gk=pltpu.VMEM((T, HL * D), BF16),
    gv=pltpu.VMEM((T, HL * D), BF16),
    gl=pltpu.VMEM((6, HL, T), F32),
    lam_rows=pltpu.VMEM((D, T), F32),
    lam_cols=pltpu.VMEM((T, D), F32),
    lam_wide=pltpu.VMEM((6, T, HL * D), F32),
    prefix=pltpu.VMEM((HL * NC, D, D), BF16),
    local=pltpu.VMEM((T, HL * D), F32),
    reads=pltpu.VMEM((HL, T, 5 * D), F32),
    out=pltpu.VMEM((T, HL * D), F32),
    kept_t=pltpu.VMEM((HL * NC, C, C), BF16),
    q_t=pltpu.VMEM((HL, D, T), BF16),
    bcat=pltpu.VMEM((HL, D, 5 * D), BF16),
    fcat=pltpu.VMEM((HL, T, 5 * D), BF16),
    e=pltpu.VMEM((T, HL * D), BF16),
    do=pltpu.VMEM((T, HL * D), BF16),
    ds=pltpu.VMEM((HL * NC, D, D), F32),
    stat_cols=pltpu.VMEM((T, D), F32),
    h_own=pltpu.VMEM((HL, D, D), F32),
    h_y=pltpu.VMEM((NY, D, D), F32),
    t_own=pltpu.VMEM((D, D), F32),
    a_own=pltpu.VMEM((D, D), F32),
    t_z=pltpu.VMEM((NZ, SUB, D), F32),
    pair_z=pltpu.VMEM((2, SUB, D), F32),
    quad_z=pltpu.VMEM((SUB, D), F32),
    b_own=pltpu.VMEM((3, D, D), F32),
    b_all=pltpu.VMEM((5, HL, D, D), F32),
    stat_own=pltpu.VMEM((8, T), F32),
    stat_all=pltpu.VMEM((NH, 8, T), F32),
    db=pltpu.VMEM((5, HL, D, D), F32),
    db_y=pltpu.VMEM((5, NY, D, D), F32),
    u_own=pltpu.VMEM((3, D, D), F32),
    u_z=pltpu.VMEM((3, NZ, SUB, D), F32),
    g_z=pltpu.VMEM((NZ, SUB, D), F32),
    g_own=pltpu.VMEM((D, D), F32),
    dh_own=pltpu.VMEM((NY, D, D), F32),
    dh=pltpu.VMEM((HL, D, D), F32),
    gg_own=pltpu.VMEM((8, HL * D), F32),
    gg_y=pltpu.VMEM((NY, 8, HL * D), F32),
    gg_mid=pltpu.VMEM((8, HL * D), F32),
    gg_z=pltpu.VMEM((NZ, 8, HL * D), F32),
    gg=pltpu.VMEM((1, HL * D), F32),
    sem_in=pltpu.SemaphoreType.DMA((6,)),
    sem_out=pltpu.SemaphoreType.DMA((6,)),
    s_hy=pltpu.SemaphoreType.DMA((NY,)),
    r_hy=pltpu.SemaphoreType.DMA((NY,)),
    s_by=pltpu.SemaphoreType.DMA((2, NY)),
    r_by=pltpu.SemaphoreType.DMA((2, NY)),
    s_tz=pltpu.SemaphoreType.DMA((NZ,)),
    r_tz=pltpu.SemaphoreType.DMA((NZ,)),
    s_bz=pltpu.SemaphoreType.DMA((3, NZ)),
    r_bz=pltpu.SemaphoreType.DMA((3, NZ)),
    s_ba=pltpu.SemaphoreType.DMA((3, NY)),
    r_ba=pltpu.SemaphoreType.DMA((3, NY)),
    s_st=pltpu.SemaphoreType.DMA((NH,)),
    r_st=pltpu.SemaphoreType.DMA((NH,)),
    s_db=pltpu.SemaphoreType.DMA((5, NY)),
    r_db=pltpu.SemaphoreType.DMA((5, NY)),
    s_uz=pltpu.SemaphoreType.DMA((3, NZ)),
    r_uz=pltpu.SemaphoreType.DMA((3, NZ)),
    s_gz=pltpu.SemaphoreType.DMA((NZ,)),
    r_gz=pltpu.SemaphoreType.DMA((NZ,)),
    s_dh=pltpu.SemaphoreType.DMA((NY,)),
    r_dh=pltpu.SemaphoreType.DMA((NY,)),
    s_ggy=pltpu.SemaphoreType.DMA((NY,)),
    r_ggy=pltpu.SemaphoreType.DMA((NY,)),
    s_ggz=pltpu.SemaphoreType.DMA((NZ,)),
    r_ggz=pltpu.SemaphoreType.DMA((NZ,)),
)


class Refs:
    def __init__(self, refs):
        for name, ref in zip(SCRATCH, refs, strict=True):
            setattr(self, name, ref)


def sub_rows(z):
    return pl.ds(pl.multiple_of(z * SUB, SUB), SUB)


def kernel(q_h, k_h, v_h, lam_h, gain_h, cot_h, mixed_h, gq_h, gk_h, gv_h, gl_h, gg_h, *refs):
    r = Refs(refs)
    seq = lax.axis_index("seq")
    head = lax.axis_index("head")
    y = lax.rem(seq, NY)
    z = seq // NY
    zbit = [lax.rem(z // 2**b, 2) == 1 for b in range(3)]
    y_odd = lax.rem(y, 2) == 1
    y_high = y >= 2

    at_y = lambda other: (z * NY + other, head)
    at_z = lambda other: (other * NY + y, head)
    at_head = lambda other: (seq, other)

    sent = []

    def send(cond, src, dst, s_sem, r_sem, device):
        def make():
            return pltpu.make_async_remote_copy(
                src_ref=src,
                dst_ref=dst,
                send_sem=s_sem,
                recv_sem=r_sem,
                device_id=device,
                device_id_type=MESH,
            )

        when(cond, lambda: make().start())
        sent.append((cond, make))

    def receive(cond, dst, s_sem, r_sem, device):
        def wait():
            pltpu.make_async_remote_copy(
                src_ref=dst,
                dst_ref=dst,
                send_sem=s_sem,
                recv_sem=r_sem,
                device_id=device,
                device_id_type=MESH,
            ).wait_recv()

        when(cond, wait)

    ins = [
        pltpu.make_async_copy(src, dst, r.sem_in.at[i])
        for i, (src, dst) in enumerate(
            [(k_h, r.k), (v_h, r.v), (q_h, r.q), (lam_h, r.lam), (cot_h, r.cot), (gain_h, r.gain)]
        )
    ]
    for copy in ins:
        copy.start()

    barrier = pltpu.get_barrier_semaphore()

    def greet(cond, device):
        when(
            cond,
            lambda: pl.semaphore_signal(barrier, inc=1, device_id=device, device_id_type=MESH),
        )

    for other in range(NY):
        greet(y != other, at_y(other))
    for other in range(NZ):
        greet(z != other, at_z(other))
    for other in range(NH):
        greet(head != other, at_head(other))

    ins[0].wait()
    ins[1].wait()
    for h in range(HL):
        acc = jnp.zeros((D, D), F32)
        for c in range(NC):
            r.prefix[h * NC + c] = acc.astype(BF16)
            rows = slice(c * C, (c + 1) * C)
            acc = acc + dot_tn(r.k[rows, head_lanes(h)], r.v[rows, head_lanes(h)])
        r.h_own[h] = acc
    r.h_y[y] = r.h_own[y]

    pl.semaphore_wait(barrier, NY + NZ + NH - 3)

    for o in range(NY):
        send(y != o, r.h_own.at[o], r.h_y.at[y], r.s_hy.at[o], r.r_hy.at[y], at_y(o))

    causal = lambda: lax.broadcasted_iota(jnp.int32, (C, C), 0) >= lax.broadcasted_iota(
        jnp.int32, (C, C), 1
    )
    anti = lambda: lax.broadcasted_iota(jnp.int32, (C, C), 0) <= lax.broadcasted_iota(
        jnp.int32, (C, C), 1
    )

    def local_step(c, carry):
        rows = chunk_rows(c)
        for h in range(HL):
            lanes = head_lanes(h)
            qc = r.q[rows, lanes]
            kept = jnp.where(causal(), dot_nt(qc, r.k[rows, lanes]), 0.0).astype(BF16)
            r.local[rows, lanes] = dot_nn(kept, r.v[rows, lanes]) + dot_nn(
                qc, r.prefix[h * NC + c]
            )
        return carry

    ins[2].wait()
    lax.fori_loop(0, 2, local_step, 0)

    for o in range(NY):
        receive(y != o, r.h_y.at[o], r.s_hy.at[o], r.r_hy.at[o], at_y(o))
    low = r.h_y[0] + r.h_y[1]
    r.a_own[...] = low
    r.t_own[...] = low + (r.h_y[2] + r.h_y[3])
    r.t_z[z] = r.t_own[sub_rows(z), :]
    for o in range(NZ):
        send(
            z != o,
            r.t_own.at[pl.ds(o * SUB, SUB), :],
            r.t_z.at[z],
            r.s_tz.at[o],
            r.r_tz.at[z],
            at_z(o),
        )
    for o in (1, 3):
        send(y != o, r.h_y.at[o - 1], r.b_all.at[0, y], r.s_by.at[0, o], r.r_by.at[0, y], at_y(o))
    for o in (2, 3):
        send(y != o, r.a_own, r.b_all.at[1, y], r.s_by.at[1, o], r.r_by.at[1, y], at_y(o))

    @pl.when(y_odd)
    def _():
        r.b_all[0, y] = r.h_y[y - 1]

    @pl.when(y_high)
    def _():
        r.b_all[1, y] = r.a_own[...]

    lax.fori_loop(2, NC, local_step, 0)

    for o in range(NZ):
        receive(z != o, r.t_z.at[o], r.s_tz.at[o], r.r_tz.at[o], at_z(o))
    low = r.t_z[0] + r.t_z[1]
    r.pair_z[0] = low
    r.pair_z[1] = r.t_z[4] + r.t_z[5]
    r.quad_z[...] = low + (r.t_z[2] + r.t_z[3])
    level_src = lambda b, o: [r.t_z.at[o - 1], r.pair_z.at[o // 4], r.quad_z][b]
    for b in (2, 1, 0):
        for o in range(NZ):
            if o >> b & 1:
                send(
                    z != o,
                    level_src(b, o),
                    r.b_own.at[b, sub_rows(z), :],
                    r.s_bz.at[b, o],
                    r.r_bz.at[b, z],
                    at_z(o),
                )

    @pl.when(zbit[0])
    def _():
        r.b_own[0, sub_rows(z), :] = r.t_z[z - 1]

    @pl.when(zbit[1])
    def _():
        r.b_own[1, sub_rows(z), :] = r.pair_z[z // 4]

    @pl.when(zbit[2])
    def _():
        r.b_own[2, sub_rows(z), :] = r.quad_z[...]

    ins[3].wait()
    for level in range(6):
        r.lam_rows[level * HL : (level + 1) * HL, :] = r.lam[level]
    r.lam_rows[6 * HL :, :] = jnp.zeros((D - 6 * HL, T), F32)
    for c in range(T // D):
        r.lam_cols[c * D : (c + 1) * D, :] = r.lam_rows[:, c * D : (c + 1) * D].T

    def spread_step(c, carry):
        rows = chunk_rows(c, D)
        cols = r.lam_cols[rows, :]
        for level in range(6):
            for h in range(HL):
                at = level * HL + h
                r.lam_wide[level, rows, head_lanes(h)] = jnp.broadcast_to(
                    cols[:, at : at + 1], (D, D)
                )
        return carry

    lax.fori_loop(0, T // D, spread_step, 0)

    for b in (2, 1, 0):
        for o in range(NZ):
            receive(
                zbit[b] & (z != o),
                r.b_own.at[b, pl.ds(o * SUB, SUB), :],
                r.s_bz.at[b, o],
                r.r_bz.at[b, o],
                at_z(o),
            )
        for o in range(NY):
            send(
                zbit[b] & (y != o),
                r.b_own.at[b],
                r.b_all.at[b + 2, y],
                r.s_ba.at[b, o],
                r.r_ba.at[b, y],
                at_y(o),
            )

    for b, there, sources in ((0, y_odd, None), (1, y_high, None)):
        for o in range(NY):
            receive(
                there & (y != o),
                r.b_all.at[b, o],
                r.s_by.at[b, o],
                r.r_by.at[b, o],
                at_y(o),
            )

    def take_bucket(b, there):
        @pl.when(there)
        def _():
            for h in range(HL):
                r.bcat[h, :, b * D : (b + 1) * D] = r.b_all[b, h].astype(BF16)

        @pl.when(jnp.logical_not(there))
        def _():
            for h in range(HL):
                r.bcat[h, :, b * D : (b + 1) * D] = jnp.zeros((D, D), BF16)

    take_bucket(0, y_odd)
    take_bucket(1, y_high)

    def first_step(c, carry):
        rows = chunk_rows(c)
        for h in range(HL):
            lanes = head_lanes(h)
            qc = r.q[rows, lanes]
            r.kept_t[h * NC + c] = jnp.where(anti(), dot_nt(r.k[rows, lanes], qc), 0.0).astype(
                BF16
            )
            two = dot_nn(qc, r.bcat[h, :, : 2 * D])
            r.reads[h, rows, : 2 * D] = two
            r.out[rows, lanes] = (
                r.lam_wide[0, rows, lanes] * r.local[rows, lanes]
                + r.lam_wide[1, rows, lanes] * two[:, :D]
                + r.lam_wide[2, rows, lanes] * two[:, D:]
            )
        return carry

    lax.fori_loop(0, NC, first_step, 0)

    for h in range(HL):
        for c in range(NC):
            r.q_t[h, :, c * C : (c + 1) * C] = r.q[c * C : (c + 1) * C, head_lanes(h)].T

    for b in (2, 1, 0):
        for o in range(NY):
            receive(
                zbit[b] & (y != o),
                r.b_all.at[b + 2, o],
                r.s_ba.at[b, o],
                r.r_ba.at[b, o],
                at_y(o),
            )

        @pl.when(zbit[b])
        def _(b=b):
            r.b_all[b + 2, y] = r.b_own[b]

        take_bucket(b + 2, zbit[b])

    ins[4].wait()
    ins[5].wait()

    def out_step(c, carry):
        rows = chunk_rows(c)
        squares = []
        inners = []
        for h in range(HL):
            lanes = head_lanes(h)
            three = dot_nn(r.q[rows, lanes], r.bcat[h, :, 2 * D :])
            r.reads[h, rows, 2 * D :] = three
            total = r.out[rows, lanes]
            for b in range(3):
                total = (
                    total + r.lam_wide[b + 3, rows, lanes] * three[:, b * D : (b + 1) * D]
                )
            r.out[rows, lanes] = total
            weighted = r.cot[rows, lanes].astype(F32) * r.gain[:, lanes]
            squares.append((total * total).astype(BF16))
            inners.append((total * weighted).astype(BF16))
        ones = jnp.ones((8, HL * D), BF16)
        r.stat_own[0:1, rows] = dot_nt(ones, jnp.concatenate(squares, axis=1))[0:1]
        r.stat_own[1:2, rows] = dot_nt(ones, jnp.concatenate(inners, axis=1))[0:1]
        return carry

    lax.fori_loop(0, NC, out_step, 0)

    for o in range(NH):
        send(
            head != o,
            r.stat_own.at[pl.ds(0, 2), :],
            r.stat_all.at[head, pl.ds(0, 2), :],
            r.s_st.at[o],
            r.r_st.at[head],
            at_head(o),
        )
    r.stat_all[head, 0:2, :] = r.stat_own[0:2, :]
    for o in range(NH):
        receive(
            head != o,
            r.stat_all.at[o, pl.ds(0, 2), :],
            r.s_st.at[o],
            r.r_st.at[o],
            at_head(o),
        )
    stats = r.stat_all[0, 0:2, :]
    for o in range(1, NH):
        stats = stats + r.stat_all[o, 0:2, :]
    count = HL * D * NH
    scale = lax.rsqrt(stats[0:1] * (1.0 / count) + EPS)
    pull = stats[1:2] * scale * scale * (1.0 / count)
    r.lam_rows[2:3, :] = scale
    r.lam_rows[3:4, :] = pull
    for c in range(T // D):
        r.stat_cols[c * D : (c + 1) * D, :] = r.lam_rows[:, c * D : (c + 1) * D].T

    r.gg_own[...] = jnp.zeros((8, HL * D), F32)

    def grad_step(c, carry):
        rows = chunk_rows(c, D)
        cols = r.stat_cols[rows, :]
        scale = jnp.broadcast_to(cols[:, 2:3], (D, D))
        pull = jnp.broadcast_to(cols[:, 3:4], (D, D))
        for h in range(HL):
            lanes = head_lanes(h)
            total = r.out[rows, lanes]
            normed = total * scale
            gain = r.gain[:, lanes]
            cot = r.cot[rows, lanes].astype(F32)
            r.mixed[rows, lanes] = (normed * gain).astype(BF16)
            r.gg_own[:, lanes] += jnp.sum((cot * normed).reshape(D // 8, 8, D), axis=0)
            grad = ((cot * gain - total * pull) * scale).astype(BF16)
            r.do[rows, lanes] = grad
            grad = grad.astype(F32)
            r.e[rows, lanes] = (r.lam_wide[0, rows, lanes] * grad).astype(BF16)
            for b in range(5):
                r.fcat[h, rows, b * D : (b + 1) * D] = (
                    r.lam_wide[b + 1, rows, lanes] * grad
                ).astype(BF16)
        return carry

    lax.fori_loop(0, T // D, grad_step, 0)

    mixed_copy = pltpu.make_async_copy(r.mixed, mixed_h, r.sem_out.at[0])
    mixed_copy.start()

    for h in range(HL):
        res = dot_nn(r.q_t[h], r.fcat[h])
        for b in range(5):
            r.db[b, h] = res[:, b * D : (b + 1) * D]
    for b in (2, 1, 0):
        for o in range(NY):
            send(
                zbit[b] & (y != o),
                r.db.at[b + 2, o],
                r.db_y.at[b + 2, y],
                r.s_db.at[b + 2, o],
                r.r_db.at[b + 2, y],
                at_y(o),
            )
    for b, there in ((0, y_odd), (1, y_high)):
        for o in range(NY):
            send(
                there & (y != o),
                r.db.at[b, o],
                r.db_y.at[b, y],
                r.s_db.at[b, o],
                r.r_db.at[b, y],
                at_y(o),
            )
    for b in range(5):
        r.db_y[b, y] = r.db[b, y]
    r.gg_own[0:1, :] = jnp.sum(r.gg_own[...], axis=0, keepdims=True)
    for o in range(NY):
        send(
            y != o,
            r.gg_own.at[pl.ds(0, 1), :],
            r.gg_y.at[y, pl.ds(0, 1), :],
            r.s_ggy.at[o],
            r.r_ggy.at[y],
            at_y(o),
        )
    r.gg_y[y, 0:1, :] = r.gg_own[0:1, :]

    def level_step(c, carry):
        rows = chunk_rows(c)
        pick = (
            lax.broadcasted_iota(jnp.int32, (8, HL * D), 1) // D
            == lax.broadcasted_iota(jnp.int32, (8, HL * D), 0)
        ).astype(BF16)
        grad = [r.do[rows, head_lanes(h)].astype(F32) for h in range(HL)]
        for level in range(6):
            parts = []
            for h in range(HL):
                if level == 0:
                    read = r.local[rows, head_lanes(h)]
                else:
                    read = r.reads[h, rows, (level - 1) * D : level * D]
                parts.append((grad[h] * read).astype(BF16))
            r.gl[level, :, rows] = dot_nt(pick, jnp.concatenate(parts, axis=1))[0:HL]
        return carry

    def query_step(c, carry):
        rows = chunk_rows(c)
        for h in range(HL):
            lanes = head_lanes(h)
            ec = r.e[rows, lanes]
            pair = jnp.where(causal(), dot_nt(ec, r.v[rows, lanes]), 0.0).astype(BF16)
            r.gq[rows, lanes] = (
                dot_nn(pair, r.k[rows, lanes])
                + dot_nt(ec, r.prefix[h * NC + c])
                + dot_nt(r.fcat[h, rows, :], r.bcat[h])
            ).astype(BF16)
        return carry

    lax.fori_loop(0, NC, query_step, 0)
    gq_copy = pltpu.make_async_copy(r.gq, gq_h, r.sem_out.at[1])
    gq_copy.start()

    for b in (2, 1, 0):
        for o in range(NY):
            receive(
                zbit[b] & (y != o),
                r.db_y.at[b + 2, o],
                r.s_db.at[b + 2, o],
                r.r_db.at[b + 2, o],
                at_y(o),
            )

        @pl.when(zbit[b])
        def _(b=b):
            total = r.db_y[b + 2, 0] + r.db_y[b + 2, 1] + (r.db_y[b + 2, 2] + r.db_y[b + 2, 3])
            r.u_own[b] = total
            r.u_z[b, z] = r.u_own[b, sub_rows(z), :]

        for o in range(NZ):
            send(
                zbit[b] & (z != o),
                r.u_own.at[b, pl.ds(o * SUB, SUB), :],
                r.u_z.at[b, z],
                r.s_uz.at[b, o],
                r.r_uz.at[b, z],
                at_z(o),
            )
    for o in range(NY):
        receive(
            y != o, r.gg_y.at[o, pl.ds(0, 1), :], r.s_ggy.at[o], r.r_ggy.at[o], at_y(o)
        )
    r.gg_mid[0:1, :] = (r.gg_y[0, 0:1, :] + r.gg_y[1, 0:1, :]) + (
        r.gg_y[2, 0:1, :] + r.gg_y[3, 0:1, :]
    )
    for o in range(NZ):
        send(
            z != o,
            r.gg_mid.at[pl.ds(0, 1), :],
            r.gg_z.at[z, pl.ds(0, 1), :],
            r.s_ggz.at[o],
            r.r_ggz.at[z],
            at_z(o),
        )
    r.gg_z[z, 0:1, :] = r.gg_mid[0:1, :]

    lax.fori_loop(0, NC, level_step, 0)
    gl_copy = pltpu.make_async_copy(r.gl, gl_h, r.sem_out.at[2])
    gl_copy.start()

    for b in (2, 1, 0):
        for o in range(NZ):
            if o >> b & 1:
                receive(z != o, r.u_z.at[b, o], r.s_uz.at[b, o], r.r_uz.at[b, o], at_z(o))
    quad = (r.u_z[2, 4] + r.u_z[2, 5]) + (r.u_z[2, 6] + r.u_z[2, 7])
    pair_low = r.u_z[1, 2] + r.u_z[1, 3]
    pair_high = r.u_z[1, 6] + r.u_z[1, 7]
    low = pair_low + quad
    r.g_z[0] = low + r.u_z[0, 1]
    r.g_z[1] = low
    r.g_z[2] = quad + r.u_z[0, 3]
    r.g_z[3] = quad
    r.g_z[4] = pair_high + r.u_z[0, 5]
    r.g_z[5] = pair_high
    r.g_z[6] = r.u_z[0, 7]
    r.g_z[7] = jnp.zeros((SUB, D), F32)
    for o in range(NZ):
        send(
            z != o, r.g_z.at[o], r.g_own.at[sub_rows(z), :], r.s_gz.at[o], r.r_gz.at[z], at_z(o)
        )
    r.g_own[sub_rows(z), :] = r.g_z[z]

    def key_step(c, carry):
        rows = chunk_rows(c)
        for h in range(HL):
            lanes = head_lanes(h)
            ec = r.e[rows, lanes]
            pair = jnp.where(anti(), dot_nt(r.v[rows, lanes], ec), 0.0).astype(BF16)
            r.local[rows, lanes] = dot_nn(pair, r.q[rows, lanes])
            r.out[rows, lanes] = dot_nn(r.kept_t[h * NC + c], ec)
            r.ds[h * NC + c] = dot_nn(r.q_t[h, :, rows], ec)
        return carry

    lax.fori_loop(0, 2, key_step, 0)

    for b, sources in ((0, (1, 3)), (1, (2, 3))):
        for o in sources:
            receive(y != o, r.db_y.at[b, o], r.s_db.at[b, o], r.r_db.at[b, o], at_y(o))
    for o in range(NZ):
        receive(
            z != o,
            r.g_own.at[pl.ds(o * SUB, SUB), :],
            r.s_gz.at[o],
            r.r_gz.at[o],
            at_z(o),
        )
    shared = r.g_own[...]
    upper = shared + (r.db_y[1, 2] + r.db_y[1, 3])
    r.dh_own[0] = upper + r.db_y[0, 1]
    r.dh_own[1] = upper
    r.dh_own[2] = shared + r.db_y[0, 3]
    r.dh_own[3] = shared
    for o in range(NY):
        send(y != o, r.dh_own.at[o], r.dh.at[y], r.s_dh.at[o], r.r_dh.at[y], at_y(o))
    r.dh[y] = r.dh_own[y]

    lax.fori_loop(2, NC, key_step, 0)

    for o in range(NZ):
        receive(
            z != o, r.gg_z.at[o, pl.ds(0, 1), :], r.s_ggz.at[o], r.r_ggz.at[o], at_z(o)
        )
    total = r.gg_z[0, 0:1, :]
    for o in range(1, NZ):
        total = total + r.gg_z[o, 0:1, :]
    r.gg[...] = total
    gg_copy = pltpu.make_async_copy(r.gg, gg_h, r.sem_out.at[3])
    gg_copy.start()

    for o in range(NY):
        receive(y != o, r.dh.at[o], r.s_dh.at[o], r.r_dh.at[o], at_y(o))

    for h in range(HL):
        lanes = head_lanes(h)
        acc = r.dh[h]
        for c in reversed(range(NC)):
            rows = slice(c * C, (c + 1) * C)
            half = acc.astype(BF16)
            r.gk[rows, lanes] = (r.local[rows, lanes] + dot_nt(r.v[rows, lanes], half)).astype(
                BF16
            )
            r.gv[rows, lanes] = (r.out[rows, lanes] + dot_nn(r.k[rows, lanes], half)).astype(
                BF16
            )
            acc = acc + r.ds[h * NC + c]
    gk_copy = pltpu.make_async_copy(r.gk, gk_h, r.sem_out.at[4])
    gv_copy = pltpu.make_async_copy(r.gv, gv_h, r.sem_out.at[5])
    gk_copy.start()
    gv_copy.start()

    for cond, make in sent:
        when(cond, lambda make=make: make().wait_send())
    for copy in (mixed_copy, gq_copy, gl_copy, gg_copy, gk_copy, gv_copy):
        copy.wait()


def body(query, key, value, level_coef, gain, cotangent):
    anywhere = pl.BlockSpec(memory_space=pl.ANY)
    wide = jax.ShapeDtypeStruct((T, HL * D), BF16)
    mixed, gq, gk, gv, gl, gg = pl.pallas_call(
        kernel,
        out_shape=(
            wide,
            wide,
            wide,
            wide,
            jax.ShapeDtypeStruct((6, HL, T), F32),
            jax.ShapeDtypeStruct((1, HL * D), F32),
        ),
        in_specs=[anywhere] * 6,
        out_specs=(anywhere,) * 6,
        scratch_shapes=list(SCRATCH.values()),
        compiler_params=pltpu.CompilerParams(
            collective_id=0, has_side_effects=True, vmem_limit_bytes=60 * 2**20
        ),
    )(query, key, value, level_coef, gain.reshape(1, -1), cotangent)
    return mixed, gq, gk, gv, gl, gg.reshape(-1)


def solution(mesh):
    placed = (
        P("seq", "head"),
        P("seq", "head"),
        P("seq", "head"),
        P(None, "head", "seq"),
        P("head"),
        P("seq", "head"),
    )
    return jax.shard_map(
        body,
        mesh=mesh,
        in_specs=placed,
        out_specs=(
            P("seq", "head"),
            P("seq", "head"),
            P("seq", "head"),
            P("seq", "head"),
            P(None, "head", "seq"),
            P("head"),
        ),
        check_vma=False,
    )
```

```python
import jax
import jax.numpy as jnp
from jax import lax
from jax.experimental import pallas as pl
from jax.experimental.pallas import tpu as pltpu
from jax.sharding import PartitionSpec as P

EPS = 1e-06
F32 = jnp.float32
BF16 = jnp.bfloat16
MESH = pl.DeviceIdType.MESH

NY = 4
NZ = 8
NH = 8
HL = 4
D = 128
T = 1024
C = 256
NC = T // C
SUB = D // NZ


def dot_nn(a, b):
    return lax.dot_general(a, b, (((1,), (0,)), ((), ())), preferred_element_type=F32)


def dot_nt(a, b):
    return lax.dot_general(a, b, (((1,), (1,)), ((), ())), preferred_element_type=F32)


def dot_tn(a, b):
    return lax.dot_general(a, b, (((0,), (0,)), ((), ())), preferred_element_type=F32)


def head_lanes(h):
    if isinstance(h, int):
        return slice(h * D, (h + 1) * D)
    return pl.ds(pl.multiple_of(h * D, D), D)


def chunk_rows(c, size=C):
    return pl.ds(pl.multiple_of(c * size, size), size)


def when(cond, fn):
    if cond is True:
        fn()
    elif cond is not False:
        pl.when(cond)(fn)


SCRATCH = dict(
    q=pltpu.VMEM((T, HL * D), BF16),
    k=pltpu.VMEM((T, HL * D), BF16),
    v=pltpu.VMEM((T, HL * D), BF16),
    cot=pltpu.VMEM((T, HL * D), BF16),
    lam=pltpu.VMEM((6, HL, T), F32),
    gain=pltpu.VMEM((1, HL * D), F32),
    lam_rows=pltpu.VMEM((D, T), F32),
    lam_cols=pltpu.VMEM((T, D), F32),
    lam_wide=pltpu.VMEM((6, T, HL * D), F32),
    prefix=pltpu.VMEM((HL * NC, D, D), BF16),
    local=pltpu.VMEM((T, HL * D), F32),
    key_part=pltpu.VMEM((T, HL * D), F32),
    reads=pltpu.VMEM((HL, T, 5 * D), F32),
    out=pltpu.VMEM((T, HL * D), F32),
    kept_t=pltpu.VMEM((HL * NC, C, C), BF16),
    q_t=pltpu.VMEM((HL, D, T), BF16),
    bcat=pltpu.VMEM((HL, D, 5 * D), BF16),
    fcat=pltpu.VMEM((HL, T, 5 * D), BF16),
    e=pltpu.VMEM((T, HL * D), BF16),
    do=pltpu.VMEM((T, HL * D), BF16),
    ds=pltpu.VMEM((HL * NC, D, D), F32),
    stat_cols=pltpu.VMEM((T, D), F32),
    h_own=pltpu.VMEM((HL, D, D), F32),
    h_y=pltpu.VMEM((NY, D, D), F32),
    t_own=pltpu.VMEM((D, D), F32),
    a_own=pltpu.VMEM((D, D), F32),
    t_z=pltpu.VMEM((NZ, SUB, D), F32),
    pair_z=pltpu.VMEM((2, SUB, D), F32),
    quad_z=pltpu.VMEM((SUB, D), F32),
    b_own=pltpu.VMEM((3, D, D), F32),
    b_all=pltpu.VMEM((5, HL, D, D), F32),
    stat_own=pltpu.VMEM((8, T), F32),
    stat_all=pltpu.VMEM((NH, 8, T), F32),
    db=pltpu.VMEM((5, HL, D, D), F32),
    db_y=pltpu.VMEM((5, NY, D, D), F32),
    u_own=pltpu.VMEM((3, D, D), F32),
    u_z=pltpu.VMEM((3, NZ, SUB, D), F32),
    g_z=pltpu.VMEM((NZ, SUB, D), F32),
    g_own=pltpu.VMEM((D, D), F32),
    dh_own=pltpu.VMEM((NY, D, D), F32),
    dh=pltpu.VMEM((HL, D, D), F32),
    gg_own=pltpu.VMEM((8, HL * D), F32),
    gg_y=pltpu.VMEM((NY, 8, HL * D), F32),
    gg_mid=pltpu.VMEM((8, HL * D), F32),
    gg_z=pltpu.VMEM((NZ, 8, HL * D), F32),
    sem_in=pltpu.SemaphoreType.DMA((6,)),
    s_hy=pltpu.SemaphoreType.DMA((NY,)),
    r_hy=pltpu.SemaphoreType.DMA((NY,)),
    s_by=pltpu.SemaphoreType.DMA((2, NY)),
    r_by=pltpu.SemaphoreType.DMA((2, NY)),
    s_tz=pltpu.SemaphoreType.DMA((NZ,)),
    r_tz=pltpu.SemaphoreType.DMA((NZ,)),
    s_bz=pltpu.SemaphoreType.DMA((3, NZ)),
    r_bz=pltpu.SemaphoreType.DMA((3, NZ)),
    s_ba=pltpu.SemaphoreType.DMA((3, NY)),
    r_ba=pltpu.SemaphoreType.DMA((3, NY)),
    s_st=pltpu.SemaphoreType.DMA((NH,)),
    r_st=pltpu.SemaphoreType.DMA((NH,)),
    s_db=pltpu.SemaphoreType.DMA((5, NY)),
    r_db=pltpu.SemaphoreType.DMA((5, NY)),
    s_uz=pltpu.SemaphoreType.DMA((3, NZ)),
    r_uz=pltpu.SemaphoreType.DMA((3, NZ)),
    s_gz=pltpu.SemaphoreType.DMA((NZ,)),
    r_gz=pltpu.SemaphoreType.DMA((NZ,)),
    s_dh=pltpu.SemaphoreType.DMA((NY,)),
    r_dh=pltpu.SemaphoreType.DMA((NY,)),
    s_ggy=pltpu.SemaphoreType.DMA((NY,)),
    r_ggy=pltpu.SemaphoreType.DMA((NY,)),
    s_ggz=pltpu.SemaphoreType.DMA((NZ,)),
    r_ggz=pltpu.SemaphoreType.DMA((NZ,)),
)


class Refs:
    def __init__(self, refs):
        for name, ref in zip(SCRATCH, refs, strict=True):
            setattr(self, name, ref)


def sub_rows(z):
    return pl.ds(pl.multiple_of(z * SUB, SUB), SUB)


Y_TURNS = (1, 3, 2)
Z_TURNS = (4, 3, 5, 2, 6, 1, 7)
HEAD_TURNS = (4, 3, 5, 2, 6, 1, 7)


def kernel(q_h, k_h, v_h, lam_h, gain_h, cot_h, mixed_o, gq_o, gk_o, gv_o, gl_o, gg_o, *refs):
    r = Refs(refs)
    seq = lax.axis_index("seq")
    head = lax.axis_index("head")
    y = lax.rem(seq, NY)
    z = seq // NY
    bit = lambda x, b: lax.rem(x // 2**b, 2) == 1
    zbit = [bit(z, b) for b in range(3)]
    y_odd = bit(y, 0)
    y_high = y >= 2

    at_y = lambda other: (z * NY + other, head)
    at_z = lambda other: (other * NY + y, head)
    at_head = lambda other: (seq, other)
    ahead = lambda me, turn, count: lax.rem(me + turn, count)
    behind = lambda me, turn, count: lax.rem(me + count - turn, count)

    sent = []

    def send(cond, src, dst, s_sem, r_sem, device):
        def make():
            return pltpu.make_async_remote_copy(
                src_ref=src,
                dst_ref=dst,
                send_sem=s_sem,
                recv_sem=r_sem,
                device_id=device,
                device_id_type=MESH,
            )

        when(cond, lambda: make().start())
        sent.append((cond, make))

    def receive(cond, dst, s_sem, r_sem, device):
        def wait():
            pltpu.make_async_remote_copy(
                src_ref=dst,
                dst_ref=dst,
                send_sem=s_sem,
                recv_sem=r_sem,
                device_id=device,
                device_id_type=MESH,
            ).wait_recv()

        when(cond, wait)

    barrier = pltpu.get_barrier_semaphore()

    def greet(device):
        pl.semaphore_signal(barrier, inc=1, device_id=device, device_id_type=MESH)

    for d in Z_TURNS:
        greet(at_z(ahead(z, d, NZ)))
    for d in HEAD_TURNS:
        greet(at_head(ahead(head, d, NH)))
    for d in Y_TURNS:
        greet(at_y(ahead(y, d, NY)))

    ins = [
        pltpu.make_async_copy(src, dst, r.sem_in.at[i])
        for i, (src, dst) in enumerate(
            [(k_h, r.k), (v_h, r.v), (q_h, r.q), (lam_h, r.lam), (cot_h, r.cot), (gain_h, r.gain)]
        )
    ]
    for copy in ins:
        copy.start()

    ins[0].wait()
    ins[1].wait()
    for i, d in enumerate(Y_TURNS + (0,)):
        h = ahead(y, d, NY)
        lanes = head_lanes(h)
        acc = jnp.zeros((D, D), F32)
        for c in range(NC):
            r.prefix[h * NC + c] = acc.astype(BF16)
            rows = slice(c * C, (c + 1) * C)
            acc = acc + dot_tn(r.k[rows, lanes], r.v[rows, lanes])
        if d == 0:
            r.h_y[y] = acc
        else:
            r.h_own[h] = acc
            if i == 0:
                pl.semaphore_wait(barrier, NY + NZ + NH - 3)
            send(True, r.h_own.at[h], r.h_y.at[y], r.s_hy.at[d], r.r_hy.at[d], at_y(h))

    causal = lambda: lax.broadcasted_iota(jnp.int32, (C, C), 0) >= lax.broadcasted_iota(
        jnp.int32, (C, C), 1
    )
    anti = lambda: lax.broadcasted_iota(jnp.int32, (C, C), 0) <= lax.broadcasted_iota(
        jnp.int32, (C, C), 1
    )

    def local_step(c, carry):
        rows = chunk_rows(c)
        for h in range(HL):
            lanes = head_lanes(h)
            qc = r.q[rows, lanes]
            kept = jnp.where(causal(), dot_nt(qc, r.k[rows, lanes]), 0.0).astype(BF16)
            r.local[rows, lanes] = dot_nn(kept, r.v[rows, lanes]) + dot_nn(
                qc, r.prefix[h * NC + c]
            )
        return carry

    def spread_step(c, carry):
        rows = chunk_rows(c, D)
        cols = r.lam_cols[rows, :]
        for level in range(6):
            for h in range(HL):
                at = level * HL + h
                r.lam_wide[level, rows, head_lanes(h)] = jnp.broadcast_to(
                    cols[:, at : at + 1], (D, D)
                )
        return carry

    ins[2].wait()
    lax.fori_loop(0, NC, local_step, 0)
    ins[3].wait()
    for level in range(6):
        r.lam_rows[level * HL : (level + 1) * HL, :] = r.lam[level]
    r.lam_rows[6 * HL :, :] = jnp.zeros((D - 6 * HL, T), F32)
    for c in range(T // D):
        r.lam_cols[c * D : (c + 1) * D, :] = r.lam_rows[:, c * D : (c + 1) * D].T
    lax.fori_loop(0, 2, spread_step, 0)

    for d in Y_TURNS:
        o = behind(y, d, NY)
        receive(True, r.h_y.at[o], r.s_hy.at[d], r.r_hy.at[d], at_y(o))
    low = r.h_y[0] + r.h_y[1]
    r.a_own[...] = low
    r.t_own[...] = low + (r.h_y[2] + r.h_y[3])
    for d in Z_TURNS:
        o = ahead(z, d, NZ)
        send(
            True,
            r.t_own.at[sub_rows(o), :],
            r.t_z.at[z],
            r.s_tz.at[d],
            r.r_tz.at[d],
            at_z(o),
        )
    r.t_z[z] = r.t_own[sub_rows(z), :]
    for o in (1, 3):
        send(y != o, r.h_y.at[o - 1], r.b_all.at[0, y], r.s_by.at[0, o], r.r_by.at[0, y], at_y(o))
    for o in (2, 3):
        send(y != o, r.a_own, r.b_all.at[1, y], r.s_by.at[1, o], r.r_by.at[1, y], at_y(o))

    @pl.when(y_odd)
    def _():
        r.b_all[0, y] = r.h_y[y - 1]

    @pl.when(y_high)
    def _():
        r.b_all[1, y] = r.a_own[...]

    lax.fori_loop(2, T // D, spread_step, 0)

    for d in Z_TURNS:
        o = behind(z, d, NZ)
        receive(True, r.t_z.at[o], r.s_tz.at[d], r.r_tz.at[d], at_z(o))
    low = r.t_z[0] + r.t_z[1]
    r.pair_z[0] = low
    r.pair_z[1] = r.t_z[4] + r.t_z[5]
    r.quad_z[...] = low + (r.t_z[2] + r.t_z[3])
    for b in (2, 1, 0):
        for d in Z_TURNS:
            o = ahead(z, d, NZ)
            src = (r.t_z.at[lax.rem(o + NZ - 1, NZ)], r.pair_z.at[o // 4], r.quad_z)[b]
            send(
                bit(o, b),
                src,
                r.b_own.at[b, sub_rows(z), :],
                r.s_bz.at[b, d],
                r.r_bz.at[b, d],
                at_z(o),
            )

    @pl.when(zbit[0])
    def _():
        r.b_own[0, sub_rows(z), :] = r.t_z[z - 1]

    @pl.when(zbit[1])
    def _():
        r.b_own[1, sub_rows(z), :] = r.pair_z[z // 4]

    @pl.when(zbit[2])
    def _():
        r.b_own[2, sub_rows(z), :] = r.quad_z[...]

    def take_bucket(b, there):
        @pl.when(there)
        def _():
            for h in range(HL):
                r.bcat[h, :, b * D : (b + 1) * D] = r.b_all[b, h].astype(BF16)

        @pl.when(jnp.logical_not(there))
        def _():
            for h in range(HL):
                r.bcat[h, :, b * D : (b + 1) * D] = jnp.zeros((D, D), BF16)

    for b, there in ((0, y_odd), (1, y_high)):
        for o in range(NY):
            receive(
                there & (y != o),
                r.b_all.at[b, o],
                r.s_by.at[b, o],
                r.r_by.at[b, o],
                at_y(o),
            )
        take_bucket(b, there)

    def first_step(c, carry):
        rows = chunk_rows(c)
        for h in range(HL):
            lanes = head_lanes(h)
            two = dot_nn(r.q[rows, lanes], r.bcat[h, :, : 2 * D])
            r.reads[h, rows, : 2 * D] = two
            r.out[rows, lanes] = (
                r.lam_wide[0, rows, lanes] * r.local[rows, lanes]
                + r.lam_wide[1, rows, lanes] * two[:, :D]
                + r.lam_wide[2, rows, lanes] * two[:, D:]
            )
        return carry

    for b in (2, 1, 0):
        for d in Z_TURNS:
            o = behind(z, d, NZ)
            receive(
                zbit[b],
                r.b_own.at[b, sub_rows(o), :],
                r.s_bz.at[b, d],
                r.r_bz.at[b, d],
                at_z(o),
            )
        for d in Y_TURNS:
            o = ahead(y, d, NY)
            send(
                zbit[b],
                r.b_own.at[b],
                r.b_all.at[b + 2, y],
                r.s_ba.at[b, d],
                r.r_ba.at[b, d],
                at_y(o),
            )

        @pl.when(zbit[b])
        def _(b=b):
            r.b_all[b + 2, y] = r.b_own[b]

    lax.fori_loop(0, NC, first_step, 0)
    ins[4].wait()
    ins[5].wait()

    for b in (2, 1, 0):
        for d in Y_TURNS:
            o = behind(y, d, NY)
            receive(
                zbit[b],
                r.b_all.at[b + 2, o],
                r.s_ba.at[b, d],
                r.r_ba.at[b, d],
                at_y(o),
            )
        take_bucket(b + 2, zbit[b])

    def out_step(c, carry):
        rows = chunk_rows(c)
        squares = []
        inners = []
        for h in range(HL):
            lanes = head_lanes(h)
            three = dot_nn(r.q[rows, lanes], r.bcat[h, :, 2 * D :])
            r.reads[h, rows, 2 * D :] = three
            total = r.out[rows, lanes]
            for b in range(3):
                total = (
                    total + r.lam_wide[b + 3, rows, lanes] * three[:, b * D : (b + 1) * D]
                )
            r.out[rows, lanes] = total
            weighted = r.cot[rows, lanes].astype(F32) * r.gain[:, lanes]
            squares.append((total * total).astype(BF16))
            inners.append((total * weighted).astype(BF16))
        ones = jnp.ones((8, HL * D), BF16)
        r.stat_own[0:1, rows] = dot_nt(ones, jnp.concatenate(squares, axis=1))[0:1]
        r.stat_own[1:2, rows] = dot_nt(ones, jnp.concatenate(inners, axis=1))[0:1]
        return carry

    lax.fori_loop(0, NC, out_step, 0)

    for d in HEAD_TURNS:
        o = ahead(head, d, NH)
        send(
            True,
            r.stat_own.at[pl.ds(0, 2), :],
            r.stat_all.at[head, pl.ds(0, 2), :],
            r.s_st.at[d],
            r.r_st.at[d],
            at_head(o),
        )
    r.stat_all[head, 0:2, :] = r.stat_own[0:2, :]

    for h in range(HL):
        for c in range(NC):
            r.q_t[h, :, c * C : (c + 1) * C] = r.q[c * C : (c + 1) * C, head_lanes(h)].T

    def kept_step(c, carry):
        rows = chunk_rows(c)
        for h in range(HL):
            lanes = head_lanes(h)
            r.kept_t[h * NC + c] = jnp.where(
                anti(), dot_nt(r.k[rows, lanes], r.q[rows, lanes]), 0.0
            ).astype(BF16)
        return carry

    lax.fori_loop(0, NC, kept_step, 0)

    for d in HEAD_TURNS:
        o = behind(head, d, NH)
        receive(
            True,
            r.stat_all.at[o, pl.ds(0, 2), :],
            r.s_st.at[d],
            r.r_st.at[d],
            at_head(o),
        )
    stats = r.stat_all[0, 0:2, :]
    for o in range(1, NH):
        stats = stats + r.stat_all[o, 0:2, :]
    count = HL * D * NH
    scale = lax.rsqrt(stats[0:1] * (1.0 / count) + EPS)
    pull = stats[1:2] * scale * scale * (1.0 / count)
    r.lam_rows[2:3, :] = scale
    r.lam_rows[3:4, :] = pull
    for c in range(T // D):
        r.stat_cols[c * D : (c + 1) * D, :] = r.lam_rows[:, c * D : (c + 1) * D].T

    r.gg_own[...] = jnp.zeros((8, HL * D), F32)

    def grad_step(h):
        lanes = head_lanes(h)

        def step(c, carry):
            rows = chunk_rows(c, D)
            cols = r.stat_cols[rows, :]
            scale = jnp.broadcast_to(cols[:, 2:3], (D, D))
            pull = jnp.broadcast_to(cols[:, 3:4], (D, D))
            total = r.out[rows, lanes]
            normed = total * scale
            gain = r.gain[:, lanes]
            cot = r.cot[rows, lanes].astype(F32)
            mixed_o[rows, lanes] = (normed * gain).astype(BF16)
            r.gg_own[:, lanes] += jnp.sum((cot * normed).reshape(D // 8, 8, D), axis=0)
            grad = ((cot * gain - total * pull) * scale).astype(BF16)
            r.do[rows, lanes] = grad
            grad = grad.astype(F32)
            r.e[rows, lanes] = (r.lam_wide[0, rows, lanes] * grad).astype(BF16)
            for b in range(5):
                r.fcat[h, rows, b * D : (b + 1) * D] = (
                    r.lam_wide[b + 1, rows, lanes] * grad
                ).astype(BF16)
            return carry

        lax.fori_loop(0, T // D, step, 0)

    for d in Y_TURNS + (0,):
        h = ahead(y, d, NY)
        grad_step(h)
        res = dot_nn(r.q_t[h], r.fcat[h, :, 2 * D :])
        for b in range(3):
            piece = res[:, b * D : (b + 1) * D]
            if d == 0:
                r.db_y[b + 2, y] = piece
            else:
                r.db[b + 2, h] = piece
        if d:
            for b in (2, 1, 0):
                send(
                    zbit[b],
                    r.db.at[b + 2, h],
                    r.db_y.at[b + 2, y],
                    r.s_db.at[b + 2, d],
                    r.r_db.at[b + 2, d],
                    at_y(h),
                )
    for h in range(HL):
        res = dot_nn(r.q_t[h], r.fcat[h, :, : 2 * D])
        for b in range(2):
            r.db[b, h] = res[:, b * D : (b + 1) * D]
    r.gg_own[0:1, :] = jnp.sum(r.gg_own[...], axis=0, keepdims=True)

    def level_step(c, carry):
        rows = chunk_rows(c)
        pick = (
            lax.broadcasted_iota(jnp.int32, (8, HL * D), 1) // D
            == lax.broadcasted_iota(jnp.int32, (8, HL * D), 0)
        ).astype(BF16)
        grad = [r.do[rows, head_lanes(h)].astype(F32) for h in range(HL)]
        for level in range(6):
            parts = []
            for h in range(HL):
                if level == 0:
                    read = r.local[rows, head_lanes(h)]
                else:
                    read = r.reads[h, rows, (level - 1) * D : level * D]
                parts.append((grad[h] * read).astype(BF16))
            gl_o[level, :, rows] = dot_nt(pick, jnp.concatenate(parts, axis=1))[0:HL]
        return carry

    def query_step(c, carry):
        rows = chunk_rows(c)
        for h in range(HL):
            lanes = head_lanes(h)
            ec = r.e[rows, lanes]
            pair = jnp.where(causal(), dot_nt(ec, r.v[rows, lanes]), 0.0).astype(BF16)
            gq_o[rows, lanes] = (
                dot_nn(pair, r.k[rows, lanes])
                + dot_nt(ec, r.prefix[h * NC + c])
                + dot_nt(r.fcat[h, rows, :], r.bcat[h])
            ).astype(BF16)
        return carry

    def key_step(c, carry):
        rows = chunk_rows(c)
        for h in range(HL):
            lanes = head_lanes(h)
            ec = r.e[rows, lanes]
            pair = jnp.where(anti(), dot_nt(r.v[rows, lanes], ec), 0.0).astype(BF16)
            r.key_part[rows, lanes] = dot_nn(pair, r.q[rows, lanes])
            r.out[rows, lanes] = dot_nn(r.kept_t[h * NC + c], ec)
            r.ds[h * NC + c] = dot_nn(r.q_t[h, :, rows], ec)
        return carry

    lax.fori_loop(0, NC, query_step, 0)
    lax.fori_loop(0, 3, key_step, 0)

    for b in (2, 1, 0):
        for d in Y_TURNS:
            o = behind(y, d, NY)
            receive(
                zbit[b],
                r.db_y.at[b + 2, o],
                r.s_db.at[b + 2, d],
                r.r_db.at[b + 2, d],
                at_y(o),
            )

        @pl.when(zbit[b])
        def _(b=b):
            total = r.db_y[b + 2, 0] + r.db_y[b + 2, 1] + (r.db_y[b + 2, 2] + r.db_y[b + 2, 3])
            r.u_own[b] = total
            r.u_z[b, z] = r.u_own[b, sub_rows(z), :]

        for d in Z_TURNS:
            o = ahead(z, d, NZ)
            send(
                zbit[b],
                r.u_own.at[b, sub_rows(o), :],
                r.u_z.at[b, z],
                r.s_uz.at[b, d],
                r.r_uz.at[b, d],
                at_z(o),
            )
    for b, there in ((0, y_odd), (1, y_high)):
        for d in Y_TURNS:
            o = ahead(y, d, NY)
            send(
                there,
                r.db.at[b, o],
                r.db_y.at[b, y],
                r.s_db.at[b, d],
                r.r_db.at[b, d],
                at_y(o),
            )
        r.db_y[b, y] = r.db[b, y]
    for d in Y_TURNS:
        o = ahead(y, d, NY)
        send(
            True,
            r.gg_own.at[pl.ds(0, 1), :],
            r.gg_y.at[y, pl.ds(0, 1), :],
            r.s_ggy.at[d],
            r.r_ggy.at[d],
            at_y(o),
        )
    r.gg_y[y, 0:1, :] = r.gg_own[0:1, :]

    lax.fori_loop(3, NC, key_step, 0)
    lax.fori_loop(0, 2, level_step, 0)

    for b in (2, 1, 0):
        for d in Z_TURNS:
            o = behind(z, d, NZ)
            receive(bit(o, b), r.u_z.at[b, o], r.s_uz.at[b, d], r.r_uz.at[b, d], at_z(o))
    quad = (r.u_z[2, 4] + r.u_z[2, 5]) + (r.u_z[2, 6] + r.u_z[2, 7])
    pair_low = r.u_z[1, 2] + r.u_z[1, 3]
    pair_high = r.u_z[1, 6] + r.u_z[1, 7]
    low = pair_low + quad
    r.g_z[0] = low + r.u_z[0, 1]
    r.g_z[1] = low
    r.g_z[2] = quad + r.u_z[0, 3]
    r.g_z[3] = quad
    r.g_z[4] = pair_high + r.u_z[0, 5]
    r.g_z[5] = pair_high
    r.g_z[6] = r.u_z[0, 7]
    r.g_z[7] = jnp.zeros((SUB, D), F32)
    for d in Z_TURNS:
        o = ahead(z, d, NZ)
        send(
            True,
            r.g_z.at[o],
            r.g_own.at[sub_rows(z), :],
            r.s_gz.at[d],
            r.r_gz.at[d],
            at_z(o),
        )
    r.g_own[sub_rows(z), :] = r.g_z[z]

    for d in Y_TURNS:
        o = behind(y, d, NY)
        receive(True, r.gg_y.at[o, pl.ds(0, 1), :], r.s_ggy.at[d], r.r_ggy.at[d], at_y(o))
    r.gg_mid[0:1, :] = (r.gg_y[0, 0:1, :] + r.gg_y[1, 0:1, :]) + (
        r.gg_y[2, 0:1, :] + r.gg_y[3, 0:1, :]
    )
    for d in Z_TURNS:
        o = ahead(z, d, NZ)
        send(
            True,
            r.gg_mid.at[pl.ds(0, 1), :],
            r.gg_z.at[z, pl.ds(0, 1), :],
            r.s_ggz.at[d],
            r.r_ggz.at[d],
            at_z(o),
        )
    r.gg_z[z, 0:1, :] = r.gg_mid[0:1, :]

    lax.fori_loop(2, NC, level_step, 0)

    for b, sources in ((0, (1, 3)), (1, (2, 3))):
        for d in Y_TURNS:
            o = behind(y, d, NY)
            there = bit(o, b)
            receive(there, r.db_y.at[b, o], r.s_db.at[b, d], r.r_db.at[b, d], at_y(o))
    for d in Z_TURNS:
        o = behind(z, d, NZ)
        receive(True, r.g_own.at[sub_rows(o), :], r.s_gz.at[d], r.r_gz.at[d], at_z(o))
    shared = r.g_own[...]
    upper = shared + (r.db_y[1, 2] + r.db_y[1, 3])
    r.dh_own[0] = upper + r.db_y[0, 1]
    r.dh_own[1] = upper
    r.dh_own[2] = shared + r.db_y[0, 3]
    r.dh_own[3] = shared
    for d in Y_TURNS:
        o = ahead(y, d, NY)
        send(True, r.dh_own.at[o], r.dh.at[y], r.s_dh.at[d], r.r_dh.at[d], at_y(o))
    r.dh[y] = r.dh_own[y]

    for d in (0,) + Y_TURNS:
        h = behind(y, d, NY)
        lanes = head_lanes(h)
        if d:
            receive(True, r.dh.at[h], r.s_dh.at[d], r.r_dh.at[d], at_y(h))
        acc = r.dh[h]
        for c in reversed(range(NC)):
            rows = slice(c * C, (c + 1) * C)
            half = acc.astype(BF16)
            gk_o[rows, lanes] = (
                r.key_part[rows, lanes] + dot_nt(r.v[rows, lanes], half)
            ).astype(BF16)
            gv_o[rows, lanes] = (r.out[rows, lanes] + dot_nn(r.k[rows, lanes], half)).astype(
                BF16
            )
            acc = acc + r.ds[h * NC + c]

    for d in Z_TURNS:
        o = behind(z, d, NZ)
        receive(True, r.gg_z.at[o, pl.ds(0, 1), :], r.s_ggz.at[d], r.r_ggz.at[d], at_z(o))
    total = r.gg_z[0, 0:1, :]
    for o in range(1, NZ):
        total = total + r.gg_z[o, 0:1, :]
    gg_o[...] = total

    for cond, make in sent:
        when(cond, lambda make=make: make().wait_send())


def store_kernel(*refs):
    ins, outs, sem = refs[:6], refs[6:12], refs[12]
    copies = [pltpu.make_async_copy(a, b, sem.at[i]) for i, (a, b) in enumerate(zip(ins, outs))]
    for copy in copies:
        copy.start()
    for copy in copies:
        copy.wait()


def body(query, key, value, level_coef, gain, cotangent):
    anywhere = pl.BlockSpec(memory_space=pl.ANY)
    inside = pl.BlockSpec(memory_space=pltpu.VMEM)
    shapes = [((T, HL * D), BF16)] * 4 + [((6, HL, T), F32), ((1, HL * D), F32)]
    results = pl.pallas_call(
        kernel,
        out_shape=tuple(pltpu.VMEM(*shape) for shape in shapes),
        in_specs=[anywhere] * 6,
        out_specs=(inside,) * 6,
        scratch_shapes=list(SCRATCH.values()),
        compiler_params=pltpu.CompilerParams(
            collective_id=0, has_side_effects=True, vmem_limit_bytes=54 * 2**20
        ),
    )(query, key, value, level_coef, gain.reshape(1, -1), cotangent)
    mixed, gq, gk, gv, gl, gg = pl.pallas_call(
        store_kernel,
        out_shape=tuple(jax.ShapeDtypeStruct(*shape) for shape in shapes),
        in_specs=[inside] * 6,
        out_specs=(anywhere,) * 6,
        scratch_shapes=[pltpu.SemaphoreType.DMA((6,))],
        compiler_params=pltpu.CompilerParams(vmem_limit_bytes=2**20),
    )(*results)
    return mixed, gq, gk, gv, gl, gg.reshape(-1)


def solution(mesh):
    placed = (
        P("seq", "head"),
        P("seq", "head"),
        P("seq", "head"),
        P(None, "head", "seq"),
        P("head"),
        P("seq", "head"),
    )
    return jax.shard_map(
        body,
        mesh=mesh,
        in_specs=placed,
        out_specs=(
            P("seq", "head"),
            P("seq", "head"),
            P("seq", "head"),
            P("seq", "head"),
            P(None, "head", "seq"),
            P("head"),
        ),
        check_vma=False,
    )
```

```python
import jax
import jax.numpy as jnp
from jax import lax
from jax.experimental import pallas as pl
from jax.experimental.pallas import tpu as pltpu
from jax.sharding import PartitionSpec as P

EPS = 1e-06
F32 = jnp.float32
BF16 = jnp.bfloat16
MESH = pl.DeviceIdType.MESH

NY = 4
NZ = 8
NH = 8
HL = 4
D = 128
T = 1024
C = 256
NC = T // C
SUB = D // NZ


def dot_nn(a, b):
    return lax.dot_general(a, b, (((1,), (0,)), ((), ())), preferred_element_type=F32)


def dot_nt(a, b):
    return lax.dot_general(a, b, (((1,), (1,)), ((), ())), preferred_element_type=F32)


def dot_tn(a, b):
    return lax.dot_general(a, b, (((0,), (0,)), ((), ())), preferred_element_type=F32)


def head_lanes(h):
    if isinstance(h, int):
        return slice(h * D, (h + 1) * D)
    return pl.ds(pl.multiple_of(h * D, D), D)


def chunk_rows(c, size=C):
    return pl.ds(pl.multiple_of(c * size, size), size)


def when(cond, fn):
    if cond is True:
        fn()
    elif cond is not False:
        pl.when(cond)(fn)


SCRATCH = dict(
    q=pltpu.VMEM((T, HL * D), BF16),
    k=pltpu.VMEM((T, HL * D), BF16),
    v=pltpu.VMEM((T, HL * D), BF16),
    cot=pltpu.VMEM((T, HL * D), BF16),
    lam=pltpu.VMEM((6, HL, T), F32),
    gain=pltpu.VMEM((1, HL * D), F32),
    lam_rows=pltpu.VMEM((D, T), F32),
    lam_cols=pltpu.VMEM((T, D), F32),
    lam_wide=pltpu.VMEM((6, T, HL * D), F32),
    prefix=pltpu.VMEM((HL * NC, D, D), BF16),
    local=pltpu.VMEM((T, HL * D), F32),
    key_part=pltpu.VMEM((T, HL * D), F32),
    reads=pltpu.VMEM((HL, T, 5 * D), F32),
    out=pltpu.VMEM((T, HL * D), F32),
    kept_t=pltpu.VMEM((HL * NC, C, C), BF16),
    q_t=pltpu.VMEM((HL, D, T), BF16),
    bcat=pltpu.VMEM((HL, D, 5 * D), BF16),
    bhigh=pltpu.VMEM((HL, 2 * D, D), BF16),
    fcat=pltpu.VMEM((HL, T, 5 * D), BF16),
    e=pltpu.VMEM((T, HL * D), BF16),
    do=pltpu.VMEM((T, HL * D), BF16),
    ds=pltpu.VMEM((HL * NC, D, D), F32),
    stat_cols=pltpu.VMEM((T, D), F32),
    h_own=pltpu.VMEM((HL, D, D), F32),
    h_y=pltpu.VMEM((NY, D, D), F32),
    t_own=pltpu.VMEM((D, D), F32),
    a_own=pltpu.VMEM((D, D), F32),
    t_z=pltpu.VMEM((NZ, SUB, D), F32),
    pair_z=pltpu.VMEM((2, SUB, D), F32),
    quad_z=pltpu.VMEM((SUB, D), F32),
    b_own=pltpu.VMEM((3, D, D), F32),
    b_all=pltpu.VMEM((5, HL, D, D), F32),
    stat_own=pltpu.VMEM((8, T), F32),
    stat_all=pltpu.VMEM((NH, 8, T), F32),
    db=pltpu.VMEM((5, HL, D, D), F32),
    db_y=pltpu.VMEM((5, NY, D, D), F32),
    u_own=pltpu.VMEM((3, D, D), F32),
    u_z=pltpu.VMEM((3, NZ, SUB, D), F32),
    g_z=pltpu.VMEM((NZ, SUB, D), F32),
    g_own=pltpu.VMEM((D, D), F32),
    u0_in=pltpu.VMEM((D, D), F32),
    dh_own=pltpu.VMEM((NY, D, D), F32),
    dh=pltpu.VMEM((HL, D, D), F32),
    gg_own=pltpu.VMEM((8, HL * D), F32),
    gg_y=pltpu.VMEM((NY, 8, HL * D), F32),
    gg_mid=pltpu.VMEM((8, HL * D), F32),
    gg_z=pltpu.VMEM((NZ, 8, HL * D), F32),
    sem_in=pltpu.SemaphoreType.DMA((6,)),
    ring=pltpu.SemaphoreType.REGULAR((2,)),
    s_t0=pltpu.SemaphoreType.DMA((1,)),
    r_t0=pltpu.SemaphoreType.DMA((1,)),
    s_u0=pltpu.SemaphoreType.DMA((1,)),
    r_u0=pltpu.SemaphoreType.DMA((1,)),
    s_hy=pltpu.SemaphoreType.DMA((NY,)),
    r_hy=pltpu.SemaphoreType.DMA((NY,)),
    s_by=pltpu.SemaphoreType.DMA((2, NY)),
    r_by=pltpu.SemaphoreType.DMA((2, NY)),
    s_tz=pltpu.SemaphoreType.DMA((NZ,)),
    r_tz=pltpu.SemaphoreType.DMA((NZ,)),
    s_bz=pltpu.SemaphoreType.DMA((3, NZ)),
    r_bz=pltpu.SemaphoreType.DMA((3, NZ)),
    s_ba=pltpu.SemaphoreType.DMA((3, NY)),
    r_ba=pltpu.SemaphoreType.DMA((3, NY)),
    s_st=pltpu.SemaphoreType.DMA((NH,)),
    r_st=pltpu.SemaphoreType.DMA((NH,)),
    s_db=pltpu.SemaphoreType.DMA((5, NY)),
    r_db=pltpu.SemaphoreType.DMA((5, NY)),
    s_uz=pltpu.SemaphoreType.DMA((3, NZ)),
    r_uz=pltpu.SemaphoreType.DMA((3, NZ)),
    s_gz=pltpu.SemaphoreType.DMA((NZ,)),
    r_gz=pltpu.SemaphoreType.DMA((NZ,)),
    s_dh=pltpu.SemaphoreType.DMA((NY,)),
    r_dh=pltpu.SemaphoreType.DMA((NY,)),
    s_ggy=pltpu.SemaphoreType.DMA((NY,)),
    r_ggy=pltpu.SemaphoreType.DMA((NY,)),
    s_ggz=pltpu.SemaphoreType.DMA((NZ,)),
    r_ggz=pltpu.SemaphoreType.DMA((NZ,)),
)


class Refs:
    def __init__(self, refs):
        for name, ref in zip(SCRATCH, refs, strict=True):
            setattr(self, name, ref)


def sub_rows(z):
    return pl.ds(pl.multiple_of(z * SUB, SUB), SUB)


Y_TURNS = (1, 3, 2)
Z_TURNS = (4, 3, 5, 2, 6, 1, 7)
HEAD_TURNS = (4, 3, 5, 2, 6, 1, 7)


def kernel(q_h, k_h, v_h, lam_h, gain_h, cot_h, mixed_o, gq_o, gk_o, gv_o, gl_o, gg_o, *refs):
    r = Refs(refs)
    seq = lax.axis_index("seq")
    head = lax.axis_index("head")
    y = lax.rem(seq, NY)
    z = seq // NY
    bit = lambda x, b: lax.rem(x // 2**b, 2) == 1
    zbit = [bit(z, b) for b in range(3)]
    z_even = lax.rem(z, 2) == 0
    y_odd = bit(y, 0)
    y_high = y >= 2

    at_y = lambda other: (z * NY + other, head)
    at_z = lambda other: (other * NY + y, head)
    at_head = lambda other: (seq, other)
    ahead = lambda me, turn, count: lax.rem(me + turn, count)
    behind = lambda me, turn, count: lax.rem(me + count - turn, count)

    sent = []

    def send(cond, src, dst, s_sem, r_sem, device):
        def make():
            return pltpu.make_async_remote_copy(
                src_ref=src,
                dst_ref=dst,
                send_sem=s_sem,
                recv_sem=r_sem,
                device_id=device,
                device_id_type=MESH,
            )

        when(cond, lambda: make().start())
        sent.append((cond, make))

    def receive(cond, dst, s_sem, r_sem, device):
        def wait():
            pltpu.make_async_remote_copy(
                src_ref=dst,
                dst_ref=dst,
                send_sem=s_sem,
                recv_sem=r_sem,
                device_id=device,
                device_id_type=MESH,
            ).wait_recv()

        when(cond, wait)

    ins = [
        pltpu.make_async_copy(src, dst, r.sem_in.at[i])
        for i, (src, dst) in enumerate(
            [(k_h, r.k), (v_h, r.v), (q_h, r.q), (lam_h, r.lam), (cot_h, r.cot), (gain_h, r.gain)]
        )
    ]
    for copy in ins[:2]:
        copy.start()

    barrier = pltpu.get_barrier_semaphore()

    def greet(device):
        pl.semaphore_signal(barrier, inc=1, device_id=device, device_id_type=MESH)

    for d in (1, NZ - 1):
        greet(at_z(ahead(z, d, NZ)))
    for d in Y_TURNS:
        greet(at_y(ahead(y, d, NY)))
    for d in HEAD_TURNS:
        greet(at_head(ahead(head, d, NH)))

    def pass_on(step, apart):
        for d in (apart, NZ - apart):
            pl.semaphore_signal(
                r.ring.at[step],
                inc=1,
                device_id=at_z(ahead(z, d, NZ)),
                device_id_type=MESH,
            )

    ins[0].wait()
    ins[1].wait()
    for copy in ins[2:]:
        copy.start()
    for i, d in enumerate(Y_TURNS + (0,)):
        h = ahead(y, d, NY)
        lanes = head_lanes(h)
        acc = jnp.zeros((D, D), F32)
        for c in range(NC):
            r.prefix[h * NC + c] = acc.astype(BF16)
            rows = slice(c * C, (c + 1) * C)
            acc = acc + dot_tn(r.k[rows, lanes], r.v[rows, lanes])
        if d == 0:
            r.h_y[y] = acc
        else:
            r.h_own[h] = acc
            if i == 0:
                pl.semaphore_wait(barrier, NY + NH)
            send(True, r.h_own.at[h], r.h_y.at[y], r.s_hy.at[d], r.r_hy.at[d], at_y(h))

    causal = lambda: lax.broadcasted_iota(jnp.int32, (C, C), 0) >= lax.broadcasted_iota(
        jnp.int32, (C, C), 1
    )
    anti = lambda: lax.broadcasted_iota(jnp.int32, (C, C), 0) <= lax.broadcasted_iota(
        jnp.int32, (C, C), 1
    )

    def local_step(c, carry):
        rows = chunk_rows(c)
        for h in range(HL):
            lanes = head_lanes(h)
            qc = r.q[rows, lanes]
            kept = jnp.where(causal(), dot_nt(qc, r.k[rows, lanes]), 0.0).astype(BF16)
            r.local[rows, lanes] = dot_nn(kept, r.v[rows, lanes]) + dot_nn(
                qc, r.prefix[h * NC + c]
            )
        return carry

    def spread_step(c, carry):
        rows = chunk_rows(c, D)
        cols = r.lam_cols[rows, :]
        for level in range(6):
            for h in range(HL):
                at = level * HL + h
                r.lam_wide[level, rows, head_lanes(h)] = jnp.broadcast_to(
                    cols[:, at : at + 1], (D, D)
                )
        return carry

    ins[2].wait()
    pass_on(0, 1)
    lax.fori_loop(0, 2, local_step, 0)
    pl.semaphore_wait(r.ring.at[0], 2)
    pass_on(1, 2)
    lax.fori_loop(2, NC, local_step, 0)
    ins[3].wait()
    for level in range(6):
        r.lam_rows[level * HL : (level + 1) * HL, :] = r.lam[level]
    r.lam_rows[6 * HL :, :] = jnp.zeros((D - 6 * HL, T), F32)
    for c in range(T // D):
        r.lam_cols[c * D : (c + 1) * D, :] = r.lam_rows[:, c * D : (c + 1) * D].T
    lax.fori_loop(0, 2, spread_step, 0)

    for d in Y_TURNS:
        o = behind(y, d, NY)
        receive(True, r.h_y.at[o], r.s_hy.at[d], r.r_hy.at[d], at_y(o))
    low = r.h_y[0] + r.h_y[1]
    r.a_own[...] = low
    r.t_own[...] = low + (r.h_y[2] + r.h_y[3])
    pl.semaphore_wait(r.ring.at[1], 2)
    for d in Z_TURNS:
        o = ahead(z, d, NZ)
        send(
            True,
            r.t_own.at[sub_rows(o), :],
            r.t_z.at[z],
            r.s_tz.at[d],
            r.r_tz.at[d],
            at_z(o),
        )
    r.t_z[z] = r.t_own[sub_rows(z), :]
    up, down = ahead(z, 1, NZ), behind(z, 1, NZ)
    send(z_even, r.t_own, r.b_own.at[0], r.s_t0.at[0], r.r_t0.at[0], at_z(up))
    for o in (1, 3):
        send(y != o, r.h_y.at[o - 1], r.b_all.at[0, y], r.s_by.at[0, o], r.r_by.at[0, y], at_y(o))
    for o in (2, 3):
        send(y != o, r.a_own, r.b_all.at[1, y], r.s_by.at[1, o], r.r_by.at[1, y], at_y(o))

    @pl.when(y_odd)
    def _():
        r.b_all[0, y] = r.h_y[y - 1]

    @pl.when(y_high)
    def _():
        r.b_all[1, y] = r.a_own[...]

    lax.fori_loop(2, T // D, spread_step, 0)

    def share_bucket(b):
        for d in Y_TURNS:
            o = ahead(y, d, NY)
            send(
                zbit[b],
                r.b_own.at[b],
                r.b_all.at[b + 2, y],
                r.s_ba.at[b, d],
                r.r_ba.at[b, d],
                at_y(o),
            )

        @pl.when(zbit[b])
        def _():
            r.b_all[b + 2, y] = r.b_own[b]

    def receive_bucket(b):
        for d in Y_TURNS:
            o = behind(y, d, NY)
            receive(
                zbit[b],
                r.b_all.at[b + 2, o],
                r.s_ba.at[b, d],
                r.r_ba.at[b, d],
                at_y(o),
            )
        take_bucket(b + 2, zbit[b])

    receive(zbit[0], r.b_own.at[0], r.s_t0.at[0], r.r_t0.at[0], at_z(down))
    share_bucket(0)

    for d in Z_TURNS:
        o = behind(z, d, NZ)
        receive(True, r.t_z.at[o], r.s_tz.at[d], r.r_tz.at[d], at_z(o))
    low = r.t_z[0] + r.t_z[1]
    r.pair_z[0] = low
    r.pair_z[1] = r.t_z[4] + r.t_z[5]
    r.quad_z[...] = low + (r.t_z[2] + r.t_z[3])
    for b in (2, 1):
        for d in Z_TURNS:
            o = ahead(z, d, NZ)
            src = (None, r.pair_z.at[o // 4], r.quad_z)[b]
            send(
                bit(o, b),
                src,
                r.b_own.at[b, sub_rows(z), :],
                r.s_bz.at[b, d],
                r.r_bz.at[b, d],
                at_z(o),
            )

    @pl.when(zbit[1])
    def _():
        r.b_own[1, sub_rows(z), :] = r.pair_z[z // 4]

    @pl.when(zbit[2])
    def _():
        r.b_own[2, sub_rows(z), :] = r.quad_z[...]

    def take_bucket(b, there):
        @pl.when(there)
        def _():
            for h in range(HL):
                half = r.b_all[b, h].astype(BF16)
                r.bcat[h, :, b * D : (b + 1) * D] = half
                if b >= 3:
                    r.bhigh[h, (b - 3) * D : (b - 2) * D, :] = half

        @pl.when(jnp.logical_not(there))
        def _():
            for h in range(HL):
                r.bcat[h, :, b * D : (b + 1) * D] = jnp.zeros((D, D), BF16)
                if b >= 3:
                    r.bhigh[h, (b - 3) * D : (b - 2) * D, :] = jnp.zeros((D, D), BF16)

    def first_step(c, carry):
        rows = chunk_rows(c)
        for h in range(HL):
            lanes = head_lanes(h)
            three = dot_nn(r.q[rows, lanes], r.bcat[h, :, : 3 * D])
            r.reads[h, rows, : 3 * D] = three
            total = r.lam_wide[0, rows, lanes] * r.local[rows, lanes]
            for b in range(3):
                total = (
                    total + r.lam_wide[b + 1, rows, lanes] * three[:, b * D : (b + 1) * D]
                )
            r.out[rows, lanes] = total
            qf = r.q[rows, lanes].astype(F32)
            for b in range(2):
                r.fcat[h, rows, b * D : (b + 1) * D] = (
                    r.lam_wide[b + 4, rows, lanes] * qf
                ).astype(BF16)
            r.key_part[rows, lanes] = r.cot[rows, lanes].astype(F32) * r.gain[:, lanes]
        return carry

    for b in (2, 1):
        for d in Z_TURNS:
            o = behind(z, d, NZ)
            receive(
                zbit[b],
                r.b_own.at[b, sub_rows(o), :],
                r.s_bz.at[b, d],
                r.r_bz.at[b, d],
                at_z(o),
            )
        share_bucket(b)

    for b, there in ((0, y_odd), (1, y_high)):
        for o in range(NY):
            receive(
                there & (y != o),
                r.b_all.at[b, o],
                r.s_by.at[b, o],
                r.r_by.at[b, o],
                at_y(o),
            )
        take_bucket(b, there)
    receive_bucket(0)
    ins[4].wait()
    ins[5].wait()

    lax.fori_loop(0, NC, first_step, 0)

    def kept_step(c, carry):
        rows = chunk_rows(c)
        for h in range(HL):
            lanes = head_lanes(h)
            r.kept_t[h * NC + c] = jnp.where(
                anti(), dot_nt(r.k[rows, lanes], r.q[rows, lanes]), 0.0
            ).astype(BF16)
        return carry

    for b in (2, 1):
        receive_bucket(b)

    def out_step(c, carry):
        rows = chunk_rows(c)
        squares = []
        inners = []
        for h in range(HL):
            lanes = head_lanes(h)
            total = r.out[rows, lanes] + dot_nn(r.fcat[h, rows, : 2 * D], r.bhigh[h])
            r.out[rows, lanes] = total
            weighted = r.key_part[rows, lanes]
            squares.append((total * total).astype(BF16))
            inners.append((total * weighted).astype(BF16))
        ones = jnp.ones((8, HL * D), BF16)
        r.stat_own[0:1, rows] = dot_nt(ones, jnp.concatenate(squares, axis=1))[0:1]
        r.stat_own[1:2, rows] = dot_nt(ones, jnp.concatenate(inners, axis=1))[0:1]
        return carry

    lax.fori_loop(0, NC, out_step, 0)

    for d in HEAD_TURNS:
        o = ahead(head, d, NH)
        send(
            True,
            r.stat_own.at[pl.ds(0, 2), :],
            r.stat_all.at[head, pl.ds(0, 2), :],
            r.s_st.at[d],
            r.r_st.at[d],
            at_head(o),
        )
    r.stat_all[head, 0:2, :] = r.stat_own[0:2, :]

    for h in range(HL):
        for c in range(NC):
            r.q_t[h, :, c * C : (c + 1) * C] = r.q[c * C : (c + 1) * C, head_lanes(h)].T

    def high_reads_step(c, carry):
        rows = chunk_rows(c)
        for h in range(HL):
            r.reads[h, rows, 3 * D :] = dot_nn(r.q[rows, head_lanes(h)], r.bcat[h, :, 3 * D :])
        return carry

    lax.fori_loop(0, NC, high_reads_step, 0)
    lax.fori_loop(0, NC, kept_step, 0)

    for d in HEAD_TURNS:
        o = behind(head, d, NH)
        receive(
            True,
            r.stat_all.at[o, pl.ds(0, 2), :],
            r.s_st.at[d],
            r.r_st.at[d],
            at_head(o),
        )
    stats = r.stat_all[0, 0:2, :]
    for o in range(1, NH):
        stats = stats + r.stat_all[o, 0:2, :]
    count = HL * D * NH
    scale = lax.rsqrt(stats[0:1] * (1.0 / count) + EPS)
    pull = stats[1:2] * scale * scale * (1.0 / count)
    r.lam_rows[2:3, :] = scale
    r.lam_rows[3:4, :] = pull
    for c in range(T // D):
        r.stat_cols[c * D : (c + 1) * D, :] = r.lam_rows[:, c * D : (c + 1) * D].T

    r.gg_own[...] = jnp.zeros((8, HL * D), F32)

    def high_grad_step(h):
        lanes = head_lanes(h)

        def step(c, carry):
            rows = chunk_rows(c, D)
            cols = r.stat_cols[rows, :]
            scale = jnp.broadcast_to(cols[:, 2:3], (D, D))
            pull = jnp.broadcast_to(cols[:, 3:4], (D, D))
            grad = ((r.key_part[rows, lanes] - r.out[rows, lanes] * pull) * scale).astype(BF16)
            r.do[rows, lanes] = grad
            grad = grad.astype(F32)
            for b in (3, 4):
                r.fcat[h, rows, b * D : (b + 1) * D] = (
                    r.lam_wide[b + 1, rows, lanes] * grad
                ).astype(BF16)
            return carry

        lax.fori_loop(0, T // D, step, 0, unroll=2)

    def rest_step(c, carry):
        rows = chunk_rows(c, D)
        scale = jnp.broadcast_to(r.stat_cols[rows, 2:3], (D, D))
        for h in range(HL):
            lanes = head_lanes(h)
            normed = r.out[rows, lanes] * scale
            mixed_o[rows, lanes] = (normed * r.gain[:, lanes]).astype(BF16)
            cot = r.cot[rows, lanes].astype(F32)
            r.gg_own[:, lanes] += jnp.sum((cot * normed).reshape(D // 8, 8, D), axis=0)
            grad = r.do[rows, lanes].astype(F32)
            r.e[rows, lanes] = (r.lam_wide[0, rows, lanes] * grad).astype(BF16)
            for b in range(3):
                r.fcat[h, rows, b * D : (b + 1) * D] = (
                    r.lam_wide[b + 1, rows, lanes] * grad
                ).astype(BF16)
        return carry

    def send_grad(level, d, o, there):
        send(
            there,
            r.db.at[level, o],
            r.db_y.at[level, y],
            r.s_db.at[level, d],
            r.r_db.at[level, d],
            at_y(o),
        )

    def receive_grad(level, there):
        for d in Y_TURNS:
            o = behind(y, d, NY)
            receive(
                there(o),
                r.db_y.at[level, o],
                r.s_db.at[level, d],
                r.r_db.at[level, d],
                at_y(o),
            )

    for d in Y_TURNS + (0,):
        h = ahead(y, d, NY)
        high_grad_step(h)
        res = dot_nn(r.q_t[h], r.fcat[h, :, 3 * D :])
        for b in (1, 2):
            piece = res[:, (b - 1) * D : b * D]
            if d == 0:
                r.db_y[b + 2, y] = piece
            else:
                r.db[b + 2, h] = piece
        if d:
            for b in (2, 1):
                send_grad(b + 2, d, h, zbit[b])
    lax.fori_loop(0, T // D, rest_step, 0)
    for d in Y_TURNS + (0,):
        h = ahead(y, d, NY)
        res = dot_nn(r.q_t[h], r.fcat[h, :, : 3 * D])
        for b in range(3):
            piece = res[:, b * D : (b + 1) * D]
            if d == 0:
                r.db_y[b, y] = piece
            else:
                r.db[b, h] = piece
        if d:
            for b, there in ((2, zbit[0]), (1, y_high), (0, y_odd)):
                send_grad(b, d, h, there)
    r.gg_own[0:1, :] = jnp.sum(r.gg_own[...], axis=0, keepdims=True)

    def level_step(c, carry):
        rows = chunk_rows(c)
        pick = (
            lax.broadcasted_iota(jnp.int32, (8, HL * D), 1) // D
            == lax.broadcasted_iota(jnp.int32, (8, HL * D), 0)
        ).astype(BF16)
        grad = [r.do[rows, head_lanes(h)].astype(F32) for h in range(HL)]
        for level in range(6):
            parts = []
            for h in range(HL):
                if level == 0:
                    read = r.local[rows, head_lanes(h)]
                else:
                    read = r.reads[h, rows, (level - 1) * D : level * D]
                parts.append((grad[h] * read).astype(BF16))
            gl_o[level, :, rows] = dot_nt(pick, jnp.concatenate(parts, axis=1))[0:HL]
        return carry

    def query_step(c, carry):
        rows = chunk_rows(c)
        for h in range(HL):
            lanes = head_lanes(h)
            ec = r.e[rows, lanes]
            pair = jnp.where(causal(), dot_nt(ec, r.v[rows, lanes]), 0.0).astype(BF16)
            gq_o[rows, lanes] = (
                dot_nn(pair, r.k[rows, lanes])
                + dot_nt(ec, r.prefix[h * NC + c])
                + dot_nt(r.fcat[h, rows, :], r.bcat[h])
            ).astype(BF16)
        return carry

    def key_step(c, carry):
        rows = chunk_rows(c)
        for h in range(HL):
            lanes = head_lanes(h)
            ec = r.e[rows, lanes]
            pair = jnp.where(anti(), dot_nt(r.v[rows, lanes], ec), 0.0).astype(BF16)
            r.key_part[rows, lanes] = dot_nn(pair, r.q[rows, lanes])
            r.out[rows, lanes] = dot_nn(r.kept_t[h * NC + c], ec)
            r.ds[h * NC + c] = dot_nn(r.q_t[h, :, rows], ec)
        return carry

    lax.fori_loop(0, NC, query_step, 0)
    lax.fori_loop(0, 2, key_step, 0)

    def sum_over_y(level):
        return (r.db_y[level, 0] + r.db_y[level, 1]) + (r.db_y[level, 2] + r.db_y[level, 3])

    for b in (2, 1):
        receive_grad(b + 2, lambda o: zbit[b])

        @pl.when(zbit[b])
        def _(b=b):
            r.u_own[b] = sum_over_y(b + 2)
            r.u_z[b, z] = r.u_own[b, sub_rows(z), :]

        for d in Z_TURNS:
            o = ahead(z, d, NZ)
            send(
                zbit[b],
                r.u_own.at[b, sub_rows(o), :],
                r.u_z.at[b, z],
                r.s_uz.at[b, d],
                r.r_uz.at[b, d],
                at_z(o),
            )
    for d in Y_TURNS:
        o = ahead(y, d, NY)
        send(
            True,
            r.gg_own.at[pl.ds(0, 1), :],
            r.gg_y.at[y, pl.ds(0, 1), :],
            r.s_ggy.at[d],
            r.r_ggy.at[d],
            at_y(o),
        )
    r.gg_y[y, 0:1, :] = r.gg_own[0:1, :]

    lax.fori_loop(2, NC, key_step, 0)

    receive_grad(2, lambda o: zbit[0])

    @pl.when(zbit[0])
    def _():
        r.u_own[0] = sum_over_y(2)

    send(zbit[0], r.u_own.at[0], r.u0_in, r.s_u0.at[0], r.r_u0.at[0], at_z(down))
    lax.fori_loop(0, 1, level_step, 0)

    for b in (2, 1):
        for d in Z_TURNS:
            o = behind(z, d, NZ)
            receive(bit(o, b), r.u_z.at[b, o], r.s_uz.at[b, d], r.r_uz.at[b, d], at_z(o))
    quad = (r.u_z[2, 4] + r.u_z[2, 5]) + (r.u_z[2, 6] + r.u_z[2, 7])
    pair_low = r.u_z[1, 2] + r.u_z[1, 3]
    pair_high = r.u_z[1, 6] + r.u_z[1, 7]
    low = pair_low + quad
    r.g_z[0] = low
    r.g_z[1] = low
    r.g_z[2] = quad
    r.g_z[3] = quad
    r.g_z[4] = pair_high
    r.g_z[5] = pair_high
    for d in Z_TURNS:
        o = ahead(z, d, NZ)
        send(
            o < 6,
            r.g_z.at[o],
            r.g_own.at[sub_rows(z), :],
            r.s_gz.at[d],
            r.r_gz.at[d],
            at_z(o),
        )

    @pl.when(z < 6)
    def _():
        r.g_own[sub_rows(z), :] = r.g_z[z]

    @pl.when(z >= 6)
    def _():
        r.g_own[...] = jnp.zeros((D, D), F32)

    for d in Y_TURNS:
        o = behind(y, d, NY)
        receive(True, r.gg_y.at[o, pl.ds(0, 1), :], r.s_ggy.at[d], r.r_ggy.at[d], at_y(o))
    r.gg_mid[0:1, :] = (r.gg_y[0, 0:1, :] + r.gg_y[1, 0:1, :]) + (
        r.gg_y[2, 0:1, :] + r.gg_y[3, 0:1, :]
    )
    for d in Z_TURNS:
        o = ahead(z, d, NZ)
        send(
            True,
            r.gg_mid.at[pl.ds(0, 1), :],
            r.gg_z.at[z, pl.ds(0, 1), :],
            r.s_ggz.at[d],
            r.r_ggz.at[d],
            at_z(o),
        )
    r.gg_z[z, 0:1, :] = r.gg_mid[0:1, :]

    lax.fori_loop(1, NC, level_step, 0)

    for b in range(2):
        receive_grad(b, lambda o: bit(o, b))
    receive(z_even, r.u0_in, r.s_u0.at[0], r.r_u0.at[0], at_z(up))
    for d in Z_TURNS:
        o = behind(z, d, NZ)
        receive(z < 6, r.g_own.at[sub_rows(o), :], r.s_gz.at[d], r.r_gz.at[d], at_z(o))

    @pl.when(z_even)
    def _():
        r.g_own[...] += r.u0_in[...]

    shared = r.g_own[...]
    upper = shared + (r.db_y[1, 2] + r.db_y[1, 3])
    r.dh_own[0] = upper + r.db_y[0, 1]
    r.dh_own[1] = upper
    r.dh_own[2] = shared + r.db_y[0, 3]
    r.dh_own[3] = shared
    for d in Y_TURNS:
        o = ahead(y, d, NY)
        send(True, r.dh_own.at[o], r.dh.at[y], r.s_dh.at[d], r.r_dh.at[d], at_y(o))
    r.dh[y] = r.dh_own[y]

    for d in (0,) + Y_TURNS:
        h = behind(y, d, NY)
        lanes = head_lanes(h)
        if d:
            receive(True, r.dh.at[h], r.s_dh.at[d], r.r_dh.at[d], at_y(h))
        acc = r.dh[h]
        for c in reversed(range(NC)):
            rows = slice(c * C, (c + 1) * C)
            half = acc.astype(BF16)
            gk_o[rows, lanes] = (
                r.key_part[rows, lanes] + dot_nt(r.v[rows, lanes], half)
            ).astype(BF16)
            gv_o[rows, lanes] = (r.out[rows, lanes] + dot_nn(r.k[rows, lanes], half)).astype(
                BF16
            )
            acc = acc + r.ds[h * NC + c]

    for d in Z_TURNS:
        o = behind(z, d, NZ)
        receive(True, r.gg_z.at[o, pl.ds(0, 1), :], r.s_ggz.at[d], r.r_ggz.at[d], at_z(o))
    total = r.gg_z[0, 0:1, :]
    for o in range(1, NZ):
        total = total + r.gg_z[o, 0:1, :]
    gg_o[...] = total

    for cond, make in sent:
        when(cond, lambda make=make: make().wait_send())


def store_kernel(*refs):
    ins, outs, sem = refs[:6], refs[6:12], refs[12]
    copies = [pltpu.make_async_copy(a, b, sem.at[i]) for i, (a, b) in enumerate(zip(ins, outs))]
    for copy in copies:
        copy.start()
    for copy in copies:
        copy.wait()


def body(query, key, value, level_coef, gain, cotangent):
    anywhere = pl.BlockSpec(memory_space=pl.ANY)
    inside = pl.BlockSpec(memory_space=pltpu.VMEM)
    shapes = [((T, HL * D), BF16)] * 4 + [((6, HL, T), F32), ((1, HL * D), F32)]
    results = pl.pallas_call(
        kernel,
        out_shape=tuple(pltpu.VMEM(*shape) for shape in shapes),
        in_specs=[anywhere] * 6,
        out_specs=(inside,) * 6,
        scratch_shapes=list(SCRATCH.values()),
        compiler_params=pltpu.CompilerParams(
            collective_id=0, has_side_effects=True, vmem_limit_bytes=54 * 2**20
        ),
    )(query, key, value, level_coef, gain.reshape(1, -1), cotangent)
    mixed, gq, gk, gv, gl, gg = pl.pallas_call(
        store_kernel,
        out_shape=tuple(jax.ShapeDtypeStruct(*shape) for shape in shapes),
        in_specs=[inside] * 6,
        out_specs=(anywhere,) * 6,
        scratch_shapes=[pltpu.SemaphoreType.DMA((6,))],
        compiler_params=pltpu.CompilerParams(vmem_limit_bytes=2**20),
    )(*results)
    return mixed, gq, gk, gv, gl, gg.reshape(-1)


def solution(mesh):
    placed = (
        P("seq", "head"),
        P("seq", "head"),
        P("seq", "head"),
        P(None, "head", "seq"),
        P("head"),
        P("seq", "head"),
    )
    return jax.shard_map(
        body,
        mesh=mesh,
        in_specs=placed,
        out_specs=(
            P("seq", "head"),
            P("seq", "head"),
            P("seq", "head"),
            P("seq", "head"),
            P(None, "head", "seq"),
            P("head"),
        ),
        check_vma=False,
    )
```

```python
import jax
import jax.numpy as jnp
from jax import lax
from jax.experimental import pallas as pl
from jax.experimental.pallas import tpu as pltpu
from jax.sharding import PartitionSpec as P

EPS = 1e-06
F32 = jnp.float32
BF16 = jnp.bfloat16
MESH = pl.DeviceIdType.MESH

NY = 4
NZ = 8
NH = 8
HL = 4
D = 128
T = 1024
C = 256
NC = T // C
NQ = 4
SUB = D // NQ


def dot_nn(a, b):
    return lax.dot_general(a, b, (((1,), (0,)), ((), ())), preferred_element_type=F32)


def dot_nt(a, b):
    return lax.dot_general(a, b, (((1,), (1,)), ((), ())), preferred_element_type=F32)


def dot_tn(a, b):
    return lax.dot_general(a, b, (((0,), (0,)), ((), ())), preferred_element_type=F32)


def head_lanes(h):
    if isinstance(h, int):
        return slice(h * D, (h + 1) * D)
    return pl.ds(pl.multiple_of(h * D, D), D)


def chunk_rows(c, size=C):
    return pl.ds(pl.multiple_of(c * size, size), size)


def when(cond, fn):
    if cond is True:
        fn()
    elif cond is not False:
        pl.when(cond)(fn)


SCRATCH = dict(
    q=pltpu.VMEM((T, HL * D), BF16),
    k=pltpu.VMEM((T, HL * D), BF16),
    v=pltpu.VMEM((T, HL * D), BF16),
    cot=pltpu.VMEM((T, HL * D), BF16),
    lam=pltpu.VMEM((6, HL, T), F32),
    gain=pltpu.VMEM((1, HL * D), F32),
    lam_rows=pltpu.VMEM((D, T), F32),
    lam_cols=pltpu.VMEM((T, D), F32),
    lam_wide=pltpu.VMEM((6, T, HL * D), F32),
    prefix=pltpu.VMEM((HL * NC, D, D), BF16),
    local=pltpu.VMEM((T, HL * D), F32),
    key_part=pltpu.VMEM((T, HL * D), F32),
    reads=pltpu.VMEM((HL, T, 5 * D), F32),
    out=pltpu.VMEM((T, HL * D), F32),
    kept_t=pltpu.VMEM((HL * NC, C, C), BF16),
    q_t=pltpu.VMEM((HL, D, T), BF16),
    bcat=pltpu.VMEM((HL, D, 5 * D), BF16),
    bhigh=pltpu.VMEM((HL, 2 * D, D), BF16),
    fcat=pltpu.VMEM((HL, T, 5 * D), BF16),
    e=pltpu.VMEM((T, HL * D), BF16),
    do=pltpu.VMEM((T, HL * D), BF16),
    ds=pltpu.VMEM((HL * NC, D, D), F32),
    stat_cols=pltpu.VMEM((T, D), F32),
    h_own=pltpu.VMEM((HL, D, D), F32),
    h_y=pltpu.VMEM((NY, D, D), F32),
    t_own=pltpu.VMEM((D, D), F32),
    a_own=pltpu.VMEM((D, D), F32),
    t_z=pltpu.VMEM((NQ, SUB, D), F32),
    pair_z=pltpu.VMEM((SUB, D), F32),
    quad_z=pltpu.VMEM((SUB, D), F32),
    b_own=pltpu.VMEM((3, D, D), F32),
    b_all=pltpu.VMEM((5, HL, D, D), F32),
    stat_own=pltpu.VMEM((8, T), F32),
    stat_all=pltpu.VMEM((NH, 8, T), F32),
    db=pltpu.VMEM((5, HL, D, D), F32),
    db_y=pltpu.VMEM((5, NY, D, D), F32),
    u_own=pltpu.VMEM((3, D, D), F32),
    u_z=pltpu.VMEM((3, NQ, SUB, D), F32),
    g_z=pltpu.VMEM((2, SUB, D), F32),
    g_in=pltpu.VMEM((2, D, D), F32),
    g_own=pltpu.VMEM((D, D), F32),
    u0_in=pltpu.VMEM((D, D), F32),
    dh_own=pltpu.VMEM((NY, D, D), F32),
    dh=pltpu.VMEM((HL, D, D), F32),
    gg_own=pltpu.VMEM((8, HL * D), F32),
    gg_y=pltpu.VMEM((NY, 8, HL * D), F32),
    gg_mid=pltpu.VMEM((8, HL * D), F32),
    gg_z=pltpu.VMEM((NZ, 8, HL * D), F32),
    sem_in=pltpu.SemaphoreType.DMA((4,)),
    sem_kv=pltpu.SemaphoreType.DMA((2, HL)),
    ring=pltpu.SemaphoreType.REGULAR((2,)),
    s_t0=pltpu.SemaphoreType.DMA((1,)),
    r_t0=pltpu.SemaphoreType.DMA((1,)),
    s_u0=pltpu.SemaphoreType.DMA((1,)),
    r_u0=pltpu.SemaphoreType.DMA((1,)),
    s_hy=pltpu.SemaphoreType.DMA((NY,)),
    r_hy=pltpu.SemaphoreType.DMA((NY,)),
    s_by=pltpu.SemaphoreType.DMA((2, NY)),
    r_by=pltpu.SemaphoreType.DMA((2, NY)),
    s_tz=pltpu.SemaphoreType.DMA((NQ,)),
    r_tz=pltpu.SemaphoreType.DMA((NQ,)),
    s_bz=pltpu.SemaphoreType.DMA((3, NQ)),
    r_bz=pltpu.SemaphoreType.DMA((3, NQ)),
    s_ba=pltpu.SemaphoreType.DMA((3, NY)),
    r_ba=pltpu.SemaphoreType.DMA((3, NY)),
    s_st=pltpu.SemaphoreType.DMA((NH,)),
    r_st=pltpu.SemaphoreType.DMA((NH,)),
    s_db=pltpu.SemaphoreType.DMA((5, NY)),
    r_db=pltpu.SemaphoreType.DMA((5, NY)),
    s_uz=pltpu.SemaphoreType.DMA((3, NQ)),
    r_uz=pltpu.SemaphoreType.DMA((3, NQ)),
    s_gz=pltpu.SemaphoreType.DMA((2, NQ)),
    r_gz=pltpu.SemaphoreType.DMA((2, NQ)),
    s_dh=pltpu.SemaphoreType.DMA((NY,)),
    r_dh=pltpu.SemaphoreType.DMA((NY,)),
    s_ggy=pltpu.SemaphoreType.DMA((NY,)),
    r_ggy=pltpu.SemaphoreType.DMA((NY,)),
    s_ggz=pltpu.SemaphoreType.DMA((NZ,)),
    r_ggz=pltpu.SemaphoreType.DMA((NZ,)),
)


class Refs:
    def __init__(self, refs):
        for name, ref in zip(SCRATCH, refs, strict=True):
            setattr(self, name, ref)


def sub_rows(z):
    return pl.ds(pl.multiple_of(z * SUB, SUB), SUB)


Y_TURNS = (2, 1, 3)
Y_ARRIVALS = (1, 3, 2)
Z_TURNS = (4, 3, 5, 2, 6, 1, 7)
Q_TURNS = (3, 2, 1)
HEAD_TURNS = (4, 3, 5, 2, 6, 1, 7)


def kernel(q_h, k_h, v_h, lam_h, gain_h, cot_h, mixed_o, gq_o, gk_o, gv_o, gl_o, gg_o, *refs):
    r = Refs(refs)
    seq = lax.axis_index("seq")
    head = lax.axis_index("head")
    y = lax.rem(seq, NY)
    z = seq // NY
    bit = lambda x, b: lax.rem(x // 2**b, 2) == 1
    zbit = [bit(z, b) for b in range(3)]
    z_even = lax.rem(z, 2) == 0
    zi = lax.rem(z, NQ)
    quad = z // NQ
    at_quad = lambda other: ((quad * NQ + other) * NY + y, head)
    y_odd = bit(y, 0)
    y_high = y >= 2

    at_y = lambda other: (z * NY + other, head)
    at_z = lambda other: (other * NY + y, head)
    at_head = lambda other: (seq, other)
    ahead = lambda me, turn, count: lax.rem(me + turn, count)
    behind = lambda me, turn, count: lax.rem(me + count - turn, count)

    sent = []

    def send(cond, src, dst, s_sem, r_sem, device):
        def make():
            return pltpu.make_async_remote_copy(
                src_ref=src,
                dst_ref=dst,
                send_sem=s_sem,
                recv_sem=r_sem,
                device_id=device,
                device_id_type=MESH,
            )

        when(cond, lambda: make().start())
        sent.append((cond, make))

    def drain():
        for cond, make in sent:
            when(cond, lambda make=make: make().wait_send())
        sent.clear()

    def receive(cond, dst, s_sem, r_sem, device):
        def wait():
            pltpu.make_async_remote_copy(
                src_ref=dst,
                dst_ref=dst,
                send_sem=s_sem,
                recv_sem=r_sem,
                device_id=device,
                device_id_type=MESH,
            ).wait_recv()

        when(cond, wait)

    kv = {}
    for d in Y_TURNS + (0,):
        lanes = head_lanes(ahead(y, d, NY))
        kv[d] = [
            pltpu.make_async_copy(src.at[:, lanes], dst.at[:, lanes], r.sem_kv.at[i, d])
            for i, (src, dst) in enumerate([(k_h, r.k), (v_h, r.v)])
        ]
        for copy in kv[d]:
            copy.start()
    ins = [
        pltpu.make_async_copy(src, dst, r.sem_in.at[i])
        for i, (src, dst) in enumerate([(q_h, r.q), (lam_h, r.lam), (cot_h, r.cot), (gain_h, r.gain)])
    ]

    barrier = pltpu.get_barrier_semaphore()

    def greet(device):
        pl.semaphore_signal(barrier, inc=1, device_id=device, device_id_type=MESH)

    for d in (1, NZ - 1):
        greet(at_z(ahead(z, d, NZ)))
    for d in Y_TURNS:
        greet(at_y(ahead(y, d, NY)))
    for d in HEAD_TURNS:
        greet(at_head(ahead(head, d, NH)))

    def pass_on(step, apart):
        for d in (apart, NZ - apart):
            pl.semaphore_signal(
                r.ring.at[step],
                inc=1,
                device_id=at_z(ahead(z, d, NZ)),
                device_id_type=MESH,
            )

    for i, d in enumerate(Y_TURNS + (0,)):
        h = ahead(y, d, NY)
        lanes = head_lanes(h)
        for copy in kv[d]:
            copy.wait()
        if i == 0:
            for copy in ins:
                copy.start()
        acc = dot_tn(r.k[:, lanes], r.v[:, lanes])
        if d == 0:
            r.h_y[y] = acc
        else:
            r.h_own[h] = acc
            if i == 0:
                pl.semaphore_wait(barrier, NY + NH)
            send(True, r.h_own.at[h], r.h_y.at[y], r.s_hy.at[d], r.r_hy.at[d], at_y(h))

    causal = lambda: lax.broadcasted_iota(jnp.int32, (C, C), 0) >= lax.broadcasted_iota(
        jnp.int32, (C, C), 1
    )
    anti = lambda: lax.broadcasted_iota(jnp.int32, (C, C), 0) <= lax.broadcasted_iota(
        jnp.int32, (C, C), 1
    )

    def local_step(c, carry):
        rows = chunk_rows(c)
        for h in range(HL):
            lanes = head_lanes(h)
            qc = r.q[rows, lanes]
            kept = jnp.where(causal(), dot_nt(qc, r.k[rows, lanes]), 0.0).astype(BF16)
            r.local[rows, lanes] = dot_nn(kept, r.v[rows, lanes]) + dot_nn(
                qc, r.prefix[h * NC + c]
            )
        return carry

    def spread_step(c, carry):
        rows = chunk_rows(c, D)
        cols = r.lam_cols[rows, :]
        for level in range(6):
            for h in range(HL):
                at = level * HL + h
                r.lam_wide[level, rows, head_lanes(h)] = jnp.broadcast_to(
                    cols[:, at : at + 1], (D, D)
                )
        return carry

    ins[0].wait()
    pass_on(0, 1)
    for h in range(HL):
        lanes = head_lanes(h)
        acc = jnp.zeros((D, D), F32)
        for c in range(NC):
            r.prefix[h * NC + c] = acc.astype(BF16)
            if c < NC - 1:
                rows = slice(c * C, (c + 1) * C)
                acc = acc + dot_tn(r.k[rows, lanes], r.v[rows, lanes])
    lax.fori_loop(0, 2, local_step, 0)
    pl.semaphore_wait(r.ring.at[0], 2)
    pass_on(1, 2)
    lax.fori_loop(2, NC, local_step, 0)
    ins[1].wait()
    for level in range(6):
        r.lam_rows[level * HL : (level + 1) * HL, :] = r.lam[level]
    r.lam_rows[6 * HL :, :] = jnp.zeros((D - 6 * HL, T), F32)
    for c in range(T // D):
        r.lam_cols[c * D : (c + 1) * D, :] = r.lam_rows[:, c * D : (c + 1) * D].T
    lax.fori_loop(0, 2, spread_step, 0)

    for d in Y_TURNS:
        o = behind(y, d, NY)
        receive(True, r.h_y.at[o], r.s_hy.at[d], r.r_hy.at[d], at_y(o))
    low = r.h_y[0] + r.h_y[1]
    r.a_own[...] = low
    r.t_own[...] = low + (r.h_y[2] + r.h_y[3])
    pl.semaphore_wait(r.ring.at[1], 2)
    for d in Q_TURNS:
        o = ahead(zi, d, NQ)
        send(
            True,
            r.t_own.at[sub_rows(o), :],
            r.t_z.at[zi],
            r.s_tz.at[d],
            r.r_tz.at[d],
            at_quad(o),
        )
    r.t_z[zi] = r.t_own[sub_rows(zi), :]
    up, down = ahead(z, 1, NZ), behind(z, 1, NZ)
    send(z_even, r.t_own, r.b_own.at[0], r.s_t0.at[0], r.r_t0.at[0], at_z(up))
    for o in (1, 3):
        send(y != o, r.h_y.at[o - 1], r.b_all.at[0, y], r.s_by.at[0, o], r.r_by.at[0, y], at_y(o))
    for o in (2, 3):
        send(y != o, r.a_own, r.b_all.at[1, y], r.s_by.at[1, o], r.r_by.at[1, y], at_y(o))

    @pl.when(y_odd)
    def _():
        r.b_all[0, y] = r.h_y[y - 1]

    @pl.when(y_high)
    def _():
        r.b_all[1, y] = r.a_own[...]

    lax.fori_loop(2, T // D, spread_step, 0)

    def share_bucket(b):
        for d in Y_TURNS:
            o = ahead(y, d, NY)
            send(
                zbit[b],
                r.b_own.at[b],
                r.b_all.at[b + 2, y],
                r.s_ba.at[b, d],
                r.r_ba.at[b, d],
                at_y(o),
            )

        @pl.when(zbit[b])
        def _():
            r.b_all[b + 2, y] = r.b_own[b]

    def receive_bucket(b):
        for d in Y_TURNS:
            o = behind(y, d, NY)
            receive(
                zbit[b],
                r.b_all.at[b + 2, o],
                r.s_ba.at[b, d],
                r.r_ba.at[b, d],
                at_y(o),
            )
        take_bucket(b + 2, zbit[b])

    receive(zbit[0], r.b_own.at[0], r.s_t0.at[0], r.r_t0.at[0], at_z(down))
    share_bucket(0)

    for d in Q_TURNS:
        o = behind(zi, d, NQ)
        receive(True, r.t_z.at[o], r.s_tz.at[d], r.r_tz.at[d], at_quad(o))
    low = r.t_z[0] + r.t_z[1]
    r.pair_z[...] = low
    r.quad_z[...] = low + (r.t_z[2] + r.t_z[3])
    for k in range(NQ):
        send(
            quad == 0,
            r.quad_z,
            r.b_own.at[2, sub_rows(zi), :],
            r.s_bz.at[2, k],
            r.r_bz.at[2, zi],
            at_z(NQ + ahead(zi, k, NQ)),
        )
    for o in (2, 3):
        send(
            zi != o,
            r.pair_z,
            r.b_own.at[1, sub_rows(zi), :],
            r.s_bz.at[1, o],
            r.r_bz.at[1, zi],
            at_quad(o),
        )

    @pl.when(zbit[1])
    def _():
        r.b_own[1, sub_rows(zi), :] = r.pair_z[...]

    def take_bucket(b, there):
        @pl.when(there)
        def _():
            for h in range(HL):
                half = r.b_all[b, h].astype(BF16)
                r.bcat[h, :, b * D : (b + 1) * D] = half
                if b >= 3:
                    r.bhigh[h, (b - 3) * D : (b - 2) * D, :] = half

        @pl.when(jnp.logical_not(there))
        def _():
            for h in range(HL):
                r.bcat[h, :, b * D : (b + 1) * D] = jnp.zeros((D, D), BF16)
                if b >= 3:
                    r.bhigh[h, (b - 3) * D : (b - 2) * D, :] = jnp.zeros((D, D), BF16)

    def first_step(c, carry):
        rows = chunk_rows(c)
        for h in range(HL):
            lanes = head_lanes(h)
            three = dot_nn(r.q[rows, lanes], r.bcat[h, :, : 3 * D])
            r.reads[h, rows, : 3 * D] = three
            total = r.lam_wide[0, rows, lanes] * r.local[rows, lanes]
            for b in range(3):
                total = (
                    total + r.lam_wide[b + 1, rows, lanes] * three[:, b * D : (b + 1) * D]
                )
            r.out[rows, lanes] = total
            qf = r.q[rows, lanes].astype(F32)
            for b in range(2):
                r.fcat[h, rows, b * D : (b + 1) * D] = (
                    r.lam_wide[b + 4, rows, lanes] * qf
                ).astype(BF16)
            r.key_part[rows, lanes] = r.cot[rows, lanes].astype(F32) * r.gain[:, lanes]
        return carry

    for b in (2, 1):
        for o in range(NQ):
            receive(
                zbit[2] if b == 2 else zbit[1] & (zi != o),
                r.b_own.at[b, sub_rows(o), :],
                r.s_bz.at[b, o],
                r.r_bz.at[b, o],
                at_quad(o),
            )
        share_bucket(b)

    for b, there in ((0, y_odd), (1, y_high)):
        for o in range(NY):
            receive(
                there & (y != o),
                r.b_all.at[b, o],
                r.s_by.at[b, o],
                r.r_by.at[b, o],
                at_y(o),
            )
        take_bucket(b, there)
    receive_bucket(0)
    ins[2].wait()
    ins[3].wait()

    lax.fori_loop(0, NC, first_step, 0)

    def kept_step(c, carry):
        rows = chunk_rows(c)
        for h in range(HL):
            lanes = head_lanes(h)
            r.kept_t[h * NC + c] = jnp.where(
                anti(), dot_nt(r.k[rows, lanes], r.q[rows, lanes]), 0.0
            ).astype(BF16)
        return carry

    for b in (2, 1):
        receive_bucket(b)

    def out_step(c, carry):
        rows = chunk_rows(c)
        squares = []
        inners = []
        for h in range(HL):
            lanes = head_lanes(h)
            total = r.out[rows, lanes] + dot_nn(r.fcat[h, rows, : 2 * D], r.bhigh[h])
            r.out[rows, lanes] = total
            weighted = r.key_part[rows, lanes]
            squares.append((total * total).astype(BF16))
            inners.append((total * weighted).astype(BF16))
        ones = jnp.ones((8, HL * D), BF16)
        r.stat_own[0:1, rows] = dot_nt(ones, jnp.concatenate(squares, axis=1))[0:1]
        r.stat_own[1:2, rows] = dot_nt(ones, jnp.concatenate(inners, axis=1))[0:1]
        return carry

    lax.fori_loop(0, NC, out_step, 0, unroll=True)

    for d in HEAD_TURNS:
        o = ahead(head, d, NH)
        send(
            True,
            r.stat_own.at[pl.ds(0, 2), :],
            r.stat_all.at[head, pl.ds(0, 2), :],
            r.s_st.at[d],
            r.r_st.at[d],
            at_head(o),
        )
    r.stat_all[head, 0:2, :] = r.stat_own[0:2, :]

    for h in range(HL):
        for c in range(NC):
            r.q_t[h, :, c * C : (c + 1) * C] = r.q[c * C : (c + 1) * C, head_lanes(h)].T

    def high_reads_step(c, carry):
        rows = chunk_rows(c)
        for h in range(HL):
            r.reads[h, rows, 3 * D :] = dot_nn(r.q[rows, head_lanes(h)], r.bcat[h, :, 3 * D :])
        return carry

    later, sent[:] = sent[-len(HEAD_TURNS) :], sent[: -len(HEAD_TURNS)]
    drain()
    sent += later
    lax.fori_loop(0, NC, high_reads_step, 0)
    lax.fori_loop(0, NC, kept_step, 0)

    for d in HEAD_TURNS:
        o = behind(head, d, NH)
        receive(
            True,
            r.stat_all.at[o, pl.ds(0, 2), :],
            r.s_st.at[d],
            r.r_st.at[d],
            at_head(o),
        )
    stats = r.stat_all[0, 0:2, :]
    for o in range(1, NH):
        stats = stats + r.stat_all[o, 0:2, :]
    count = HL * D * NH
    scale = lax.rsqrt(stats[0:1] * (1.0 / count) + EPS)
    pull = stats[1:2] * scale * scale * (1.0 / count)
    r.lam_rows[2:3, :] = scale
    r.lam_rows[3:4, :] = pull
    for c in range(T // D):
        r.stat_cols[c * D : (c + 1) * D, :] = r.lam_rows[:, c * D : (c + 1) * D].T

    r.gg_own[...] = jnp.zeros((8, HL * D), F32)

    def high_grad_step(h):
        lanes = head_lanes(h)

        def step(c, carry):
            rows = chunk_rows(c, D)
            cols = r.stat_cols[rows, :]
            scale = jnp.broadcast_to(cols[:, 2:3], (D, D))
            pull = jnp.broadcast_to(cols[:, 3:4], (D, D))
            grad = ((r.key_part[rows, lanes] - r.out[rows, lanes] * pull) * scale).astype(BF16)
            r.do[rows, lanes] = grad
            grad = grad.astype(F32)
            for b in (3, 4):
                r.fcat[h, rows, b * D : (b + 1) * D] = (
                    r.lam_wide[b + 1, rows, lanes] * grad
                ).astype(BF16)
            return carry

        lax.fori_loop(0, T // D, step, 0, unroll=2)

    def rest_step(c, carry):
        rows = chunk_rows(c, D)
        scale = jnp.broadcast_to(r.stat_cols[rows, 2:3], (D, D))
        for h in range(HL):
            lanes = head_lanes(h)
            normed = r.out[rows, lanes] * scale
            mixed_o[rows, lanes] = (normed * r.gain[:, lanes]).astype(BF16)
            cot = r.cot[rows, lanes].astype(F32)
            r.gg_own[:, lanes] += jnp.sum((cot * normed).reshape(D // 8, 8, D), axis=0)
            grad = r.do[rows, lanes].astype(F32)
            r.e[rows, lanes] = (r.lam_wide[0, rows, lanes] * grad).astype(BF16)
            for b in range(3):
                r.fcat[h, rows, b * D : (b + 1) * D] = (
                    r.lam_wide[b + 1, rows, lanes] * grad
                ).astype(BF16)
        return carry

    def send_grad(level, d, o, there):
        send(
            there,
            r.db.at[level, o],
            r.db_y.at[level, y],
            r.s_db.at[level, d],
            r.r_db.at[level, d],
            at_y(o),
        )

    def receive_grad(level, there):
        for d in Y_TURNS:
            o = behind(y, d, NY)
            receive(
                there(o),
                r.db_y.at[level, o],
                r.s_db.at[level, d],
                r.r_db.at[level, d],
                at_y(o),
            )

    for d in Y_TURNS + (0,):
        h = ahead(y, d, NY)
        high_grad_step(h)
        res = dot_nn(r.q_t[h], r.fcat[h, :, 3 * D :])
        for b in (1, 2):
            piece = res[:, (b - 1) * D : b * D]
            if d == 0:
                r.db_y[b + 2, y] = piece
            else:
                r.db[b + 2, h] = piece
        if d:
            for b in (2, 1):
                send_grad(b + 2, d, h, zbit[b])
    lax.fori_loop(0, T // D, rest_step, 0)
    for d in Y_TURNS + (0,):
        h = ahead(y, d, NY)
        res = dot_nn(r.q_t[h], r.fcat[h, :, : 3 * D])
        for b in range(3):
            piece = res[:, b * D : (b + 1) * D]
            if d == 0:
                r.db_y[b, y] = piece
            else:
                r.db[b, h] = piece
        if d:
            for b, there in ((2, zbit[0]), (1, y_high), (0, y_odd)):
                send_grad(b, d, h, there)
    r.gg_own[0:1, :] = jnp.sum(r.gg_own[...], axis=0, keepdims=True)

    def level_step(c, carry):
        rows = chunk_rows(c)
        pick = (
            lax.broadcasted_iota(jnp.int32, (8, HL * D), 1) // D
            == lax.broadcasted_iota(jnp.int32, (8, HL * D), 0)
        ).astype(BF16)
        grad = [r.do[rows, head_lanes(h)].astype(F32) for h in range(HL)]
        for level in range(6):
            parts = []
            for h in range(HL):
                if level == 0:
                    read = r.local[rows, head_lanes(h)]
                else:
                    read = r.reads[h, rows, (level - 1) * D : level * D]
                parts.append((grad[h] * read).astype(BF16))
            gl_o[level, :, rows] = dot_nt(pick, jnp.concatenate(parts, axis=1))[0:HL]
        return carry

    def query_step(c, carry):
        rows = chunk_rows(c)
        for h in range(HL):
            lanes = head_lanes(h)
            ec = r.e[rows, lanes]
            pair = jnp.where(causal(), dot_nt(ec, r.v[rows, lanes]), 0.0).astype(BF16)
            gq_o[rows, lanes] = (
                dot_nn(pair, r.k[rows, lanes])
                + dot_nt(ec, r.prefix[h * NC + c])
                + dot_nt(r.fcat[h, rows, :], r.bcat[h])
            ).astype(BF16)
        return carry

    def key_step(c, carry):
        rows = chunk_rows(c)
        for h in range(HL):
            lanes = head_lanes(h)
            ec = r.e[rows, lanes]
            pair = jnp.where(anti(), dot_nt(r.v[rows, lanes], ec), 0.0).astype(BF16)
            r.key_part[rows, lanes] = dot_nn(pair, r.q[rows, lanes])
            r.out[rows, lanes] = dot_nn(r.kept_t[h * NC + c], ec)
            r.ds[h * NC + c] = dot_nn(r.q_t[h, :, rows], ec)
        return carry

    lax.fori_loop(0, 2, key_step, 0)

    def sum_over_y(level):
        return (r.db_y[level, 0] + r.db_y[level, 1]) + (r.db_y[level, 2] + r.db_y[level, 3])

    for b in (2, 1):
        receive_grad(b + 2, lambda o: zbit[b])

        @pl.when(zbit[b])
        def _(b=b):
            r.u_own[b] = sum_over_y(b + 2)
            r.u_z[b, zi] = r.u_own[b, sub_rows(zi), :]

        for d in Q_TURNS:
            o = ahead(zi, d, NQ)
            send(
                zbit[b],
                r.u_own.at[b, sub_rows(o), :],
                r.u_z.at[b, zi],
                r.s_uz.at[b, d],
                r.r_uz.at[b, d],
                at_quad(o),
            )
    for d in Y_TURNS:
        o = ahead(y, d, NY)
        send(
            True,
            r.gg_own.at[pl.ds(0, 1), :],
            r.gg_y.at[y, pl.ds(0, 1), :],
            r.s_ggy.at[d],
            r.r_ggy.at[d],
            at_y(o),
        )
    r.gg_y[y, 0:1, :] = r.gg_own[0:1, :]

    lax.fori_loop(0, 2, query_step, 0)

    receive_grad(2, lambda o: zbit[0])

    @pl.when(zbit[0])
    def _():
        r.u_own[0] = sum_over_y(2)

    send(zbit[0], r.u_own.at[0], r.u0_in, r.s_u0.at[0], r.r_u0.at[0], at_z(down))
    lax.fori_loop(2, NC, query_step, 0)

    for b in (2, 1):
        for d in Q_TURNS:
            o = behind(zi, d, NQ)
            receive(
                zbit[2] if b == 2 else bit(o, 1),
                r.u_z.at[b, o],
                r.s_uz.at[b, d],
                r.r_uz.at[b, d],
                at_quad(o),
            )

    @pl.when(zbit[2])
    def _():
        r.g_z[1] = (r.u_z[2, 0] + r.u_z[2, 1]) + (r.u_z[2, 2] + r.u_z[2, 3])

    for k in range(NQ):
        send(
            zbit[2],
            r.g_z.at[1],
            r.g_in.at[1, sub_rows(zi), :],
            r.s_gz.at[1, k],
            r.r_gz.at[1, zi],
            at_z(ahead(zi, k, NQ)),
        )
    r.g_z[0] = r.u_z[1, 2] + r.u_z[1, 3]
    for o in (0, 1):
        send(
            zi != o,
            r.g_z.at[0],
            r.g_in.at[0, sub_rows(zi), :],
            r.s_gz.at[0, o],
            r.r_gz.at[0, zi],
            at_quad(o),
        )

    @pl.when(zi < 2)
    def _():
        r.g_in[0, sub_rows(zi), :] = r.g_z[0]

    for d in Y_TURNS:
        o = behind(y, d, NY)
        receive(True, r.gg_y.at[o, pl.ds(0, 1), :], r.s_ggy.at[d], r.r_ggy.at[d], at_y(o))
    r.gg_mid[0:1, :] = (r.gg_y[0, 0:1, :] + r.gg_y[1, 0:1, :]) + (
        r.gg_y[2, 0:1, :] + r.gg_y[3, 0:1, :]
    )
    for d in Z_TURNS:
        o = ahead(z, d, NZ)
        send(
            True,
            r.gg_mid.at[pl.ds(0, 1), :],
            r.gg_z.at[z, pl.ds(0, 1), :],
            r.s_ggz.at[d],
            r.r_ggz.at[d],
            at_z(o),
        )
    r.gg_z[z, 0:1, :] = r.gg_mid[0:1, :]

    lax.fori_loop(2, NC, key_step, 0)
    lax.fori_loop(0, 2, level_step, 0)

    for b in range(2):
        receive_grad(b, lambda o: bit(o, b))
    receive(z_even, r.u0_in, r.s_u0.at[0], r.r_u0.at[0], at_z(up))
    for o in range(NQ):
        receive(
            (zi < 2) & (zi != o),
            r.g_in.at[0, sub_rows(o), :],
            r.s_gz.at[0, o],
            r.r_gz.at[0, o],
            at_quad(o),
        )
    for o in range(NQ):
        receive(
            quad == 0,
            r.g_in.at[1, sub_rows(o), :],
            r.s_gz.at[1, o],
            r.r_gz.at[1, o],
            at_z(o),
        )
    r.g_own[...] = jnp.zeros((D, D), F32)

    @pl.when(zi < 2)
    def _():
        r.g_own[...] += r.g_in[0]

    @pl.when(quad == 0)
    def _():
        r.g_own[...] += r.g_in[1]

    @pl.when(z_even)
    def _():
        r.g_own[...] += r.u0_in[...]

    shared = r.g_own[...]
    upper = shared + (r.db_y[1, 2] + r.db_y[1, 3])
    r.dh_own[0] = upper + r.db_y[0, 1]
    r.dh_own[1] = upper
    r.dh_own[2] = shared + r.db_y[0, 3]
    r.dh_own[3] = shared
    for d in Y_TURNS:
        o = ahead(y, d, NY)
        send(True, r.dh_own.at[o], r.dh.at[y], r.s_dh.at[d], r.r_dh.at[d], at_y(o))
    r.dh[y] = r.dh_own[y]
    lax.fori_loop(2, NC, level_step, 0)
    later, sent[:] = sent[-len(Y_TURNS) :], sent[: -len(Y_TURNS)]
    drain()
    sent += later
    for d in Z_TURNS:
        o = behind(z, d, NZ)
        receive(True, r.gg_z.at[o, pl.ds(0, 1), :], r.s_ggz.at[d], r.r_ggz.at[d], at_z(o))
    total = r.gg_z[0, 0:1, :]
    for o in range(1, NZ):
        total = total + r.gg_z[o, 0:1, :]
    gg_o[...] = total


    for d in (0,) + Y_ARRIVALS:
        h = behind(y, d, NY)
        lanes = head_lanes(h)
        if d:
            receive(True, r.dh.at[h], r.s_dh.at[d], r.r_dh.at[d], at_y(h))
        acc = r.dh[h]
        for c in reversed(range(NC)):
            rows = slice(c * C, (c + 1) * C)
            half = acc.astype(BF16)
            gk_o[rows, lanes] = (
                r.key_part[rows, lanes] + dot_nt(r.v[rows, lanes], half)
            ).astype(BF16)
            gv_o[rows, lanes] = (r.out[rows, lanes] + dot_nn(r.k[rows, lanes], half)).astype(
                BF16
            )
            acc = acc + r.ds[h * NC + c]

    drain()


def store_kernel(*refs):
    ins, outs, sem = refs[:6], refs[6:12], refs[12]
    copies = [pltpu.make_async_copy(a, b, sem.at[i]) for i, (a, b) in enumerate(zip(ins, outs))]
    for copy in copies:
        copy.start()
    for copy in copies:
        copy.wait()


def body(query, key, value, level_coef, gain, cotangent):
    anywhere = pl.BlockSpec(memory_space=pl.ANY)
    inside = pl.BlockSpec(memory_space=pltpu.VMEM)
    shapes = [((T, HL * D), BF16)] * 4 + [((6, HL, T), F32), ((1, HL * D), F32)]
    results = pl.pallas_call(
        kernel,
        out_shape=tuple(pltpu.VMEM(*shape) for shape in shapes),
        in_specs=[anywhere] * 6,
        out_specs=(inside,) * 6,
        scratch_shapes=list(SCRATCH.values()),
        compiler_params=pltpu.CompilerParams(
            collective_id=0, has_side_effects=True, vmem_limit_bytes=54 * 2**20
        ),
    )(query, key, value, level_coef, gain.reshape(1, -1), cotangent)
    mixed, gq, gk, gv, gl, gg = pl.pallas_call(
        store_kernel,
        out_shape=tuple(jax.ShapeDtypeStruct(*shape) for shape in shapes),
        in_specs=[inside] * 6,
        out_specs=(anywhere,) * 6,
        scratch_shapes=[pltpu.SemaphoreType.DMA((6,))],
        compiler_params=pltpu.CompilerParams(vmem_limit_bytes=2**20),
    )(*results)
    return mixed, gq, gk, gv, gl, gg.reshape(-1)


def solution(mesh):
    placed = (
        P("seq", "head"),
        P("seq", "head"),
        P("seq", "head"),
        P(None, "head", "seq"),
        P("head"),
        P("seq", "head"),
    )
    return jax.shard_map(
        body,
        mesh=mesh,
        in_specs=placed,
        out_specs=(
            P("seq", "head"),
            P("seq", "head"),
            P("seq", "head"),
            P("seq", "head"),
            P(None, "head", "seq"),
            P("head"),
        ),
        check_vma=False,
    )
```
